128 devices in a mesh: tgt: 8 (over y_hi, x), src: 16 (over y_lo, z, core).
Axes of the slice: x: 4, y: 4 (y_hi: 2, y_lo: 2; y = y_hi * 2 + y_lo), z: 4, core: 2. Of those that a mesh axis runs over, the one named last changes fastest.
Arguments:
- positions: float32 [3, 32768], P(None, ('tgt', 'src')), may hold values from -6 to 6
- forces: float32 [3, 32768], P(None, ('tgt', 'src')), may hold values from -6 to 6
- neighbours: int32 [12, 32768], P(None, ('tgt', 'src')), may hold values from 0 to 255
- patch_owner: int32 [32768, 1], P(('tgt', 'src')), may hold values from 0 to 127; in each aligned block of 256 rows (0 to 255, 256 to 511, ...) at most 10 rows name the same one
- rest_length: float32 [6, 163840], P(None, ('tgt', 'src')), may hold values from 1 to 4
- moduli: float32 [2, 163840], P(None, ('tgt', 'src')), may hold values from 0.1 to 1
- rest_bend: float32 [3, 163840], P(None, ('tgt', 'src')), may hold values from -3 to 3
Outputs:
- final_positions: float32 [3, 32768], P(None, ('tgt', 'src'))
- final_velocity: float32 [3, 32768], P(None, ('tgt', 'src'))
The draws below stay inside these ranges and needn't reach their ends.
Inputs may be any that keep to these rules, and one draw needn't show every extreme that they name: patch_owner[n, 0] is a flattened device index, tgt slowest; within the 256 nodes of one device no owner is named more than 10 times, and some device names some owner exactly 10 times. `neighbours`: indices into the node's own block of 256 nodes.
All inputs are finite; a program needn't handle non-finite values.
Results may differ from the reference program's by a relative error of at most 0.0003.
Values sent between devices are 32-bit elements; how exact they have to be, the bound alone decides.
A program may use at most 64 MiB of HBM per device.

```python
import math
import jax
import jax.numpy as jnp
import numpy as np
from jax import lax

NODES_DEV = 256
STEPS = 3
CYCLE = 12
NODES = 32768
CAP = 10
ALL_SLOTS = 163840
N_TGT = 8
N_SRC = 16
DEVICES = 128


def touch_ends(drawn, stream_key, smallest, largest):
    dims = drawn.shape
    index_at = [jax.random.randint(jax.random.fold_in(stream_key, axis), (), 0, dims[axis]) for axis in range(len(dims))]
    drawn = drawn.at[tuple(index_at)].set(smallest)
    longest = dims.index(max(dims))
    index_at[longest] = (index_at[longest] + 1) % dims[longest]
    return drawn.at[tuple(index_at)].set(largest)


def shard_levels(stream_key, extent, cuts, low, largest):
    def one(axis_at, shards_of):
        heights = jax.random.uniform(jax.random.fold_in(jax.random.fold_in(stream_key, 6), axis_at), (shards_of,), jnp.float32, low / len(cuts), largest / len(cuts))
        return jnp.repeat(jnp.exp(heights), extent[axis_at] // shards_of).reshape((-1,) + (1,) * (len(extent) - axis_at - 1))

    gain = one(*cuts[0])
    for cut in cuts[1:]:
        gain = gain * one(*cut)
    return gain


def routed_block(key, own, number, rows, amount, top, most, skew):
    ranking = jax.random.permutation(key, amount)
    heavy_load, common = load_shares(amount, rows * top, most, skew, True), load_shares(amount, rows * top, most, skew, False)
    places = jnp.arange(amount)

    def named(tallies, offset_by):
        used = int((tallies > 0).sum())
        fixed = max(1, used // 4)
        passed = fixed + (places - fixed + offset_by * (used - fixed)) % max(1, amount - fixed)
        return jnp.zeros((amount,), jnp.int32).at[ranking[jnp.where(places < fixed, places, passed)]].set(jnp.asarray(tallies, jnp.int32))

    tallies = jnp.where(number % 4 == 0, named(heavy_load, number // 4), named(common, number - number // 4 - 1))
    mixed = jax.random.permutation(jax.random.fold_in(own, 3), amount)
    giver, taker = mixed[0:amount // 2 * 2:2], mixed[1:amount // 2 * 2:2]
    slack = jnp.minimum(tallies[giver] - 1, most - tallies[taker]) // 2
    slack = jnp.where((giver == ranking[0]) | (taker == ranking[0]) | (tallies[taker] == 0), 0, jnp.maximum(slack, 0))
    passed = jax.random.randint(jax.random.fold_in(own, 4), (amount // 2,), 0, 1 << 20) % (slack + 1)
    tallies = tallies.at[giver].add(-passed).at[taker].add(passed)
    items = jnp.searchsorted(jnp.cumsum(tallies), jnp.arange(rows * top), side="right").astype(jnp.int32)
    grid = items.reshape(top, rows).T
    grid = grid[jax.random.permutation(jax.random.fold_in(own, 1), rows)]
    offset_by = jax.random.randint(jax.random.fold_in(own, 2), (rows, 1), 0, top)
    return jnp.take_along_axis(grid, (jnp.arange(top)[None, :] + offset_by) % top, axis=1)


def load_shares(count, total, reach, skew, full):
    portions = [(1 << 20) // math.isqrt(standing ** skew) + 1 for standing in range(1, count + 1)]
    largest = reach if full else min(reach, max(-(-total // count), total * portions[0] // sum(portions)))
    least = 1 if total - largest >= count - 1 else 0
    counts, rest = [largest] + [least] * (count - 1), total - largest - least * (count - 1)
    while rest > 0:
        movable = [i for i in range(1, count) if counts[i] < largest] or [i for i in range(1, count) if counts[i] < reach]
        mass, left = sum([portions[i] for i in movable]), rest
        for i in movable:
            more = min(reach - counts[i], max(1, left * portions[i] // mass), rest)
            counts[i] = counts[i] + more
            rest = rest - more
    return np.array(counts)


def normal_values(key, dims, scale, limit, pieces=(), kind=jnp.bfloat16):
    loudness = shard_levels(key, dims, pieces, -0.22, 0.18) if pieces else 1.0
    values = jax.random.normal(key, dims, jnp.float32) * scale * loudness
    return jnp.minimum(jnp.maximum(values, -limit), limit).astype(kind)


def setup_inputs(seed: int = 0) -> dict:
    seeds = jax.random.split(jax.random.key(seed), 8)
    positions = normal_values(seeds[0], (3, NODES), 1.0, 6.0, ((1, 128),), jnp.float32)
    forces = normal_values(seeds[1], (3, NODES), 1.0, 6.0, ((1, 128),), jnp.float32)
    neighbours = touch_ends(jax.random.randint(seeds[2], (CYCLE, NODES), 0, NODES_DEV), jax.random.fold_in(seeds[2], 1), 0, NODES_DEV - 1).astype(jnp.int32)
    patch_owner_keys = jax.random.split(jax.random.fold_in(seeds[3], 1), NODES // NODES_DEV)
    patch_owner_turns = jax.random.permutation(jax.random.fold_in(seeds[3], 3), NODES // NODES_DEV)
    patch_owner = jax.vmap(lambda own, number: routed_block(jax.random.fold_in(seeds[3], 2), own, number, NODES_DEV, DEVICES, 1, CAP, 2))(patch_owner_keys, patch_owner_turns).reshape((NODES, 1))
    rest_length = jnp.clip(jnp.exp(math.log(4.0) - 1.3862944 * jax.random.uniform(seeds[4], (6, ALL_SLOTS), jnp.float32) ** shard_levels(seeds[4], (6, ALL_SLOTS), ((1, 128),), -0.2, 0.2)), 1.0, 4.0)
    moduli = jnp.clip(jnp.exp(math.log(1.0) - 2.3025851 * jax.random.uniform(seeds[5], (2, ALL_SLOTS), jnp.float32) ** shard_levels(seeds[5], (2, ALL_SLOTS), ((1, 128),), -0.2, 0.2)), 0.1, 1.0)
    rest_bend = normal_values(seeds[6], (3, ALL_SLOTS), 0.5, 3.0, ((1, 128),), jnp.float32)
    return dict(positions=positions, forces=forces, neighbours=neighbours, patch_owner=patch_owner, rest_length=rest_length, moduli=moduli, rest_bend=rest_bend)


blob_square = 0.0025
time_step = 0.5

def pick_block(length, wanted):
    return wanted if length % wanted == 0 else length

def stokes_block(target_pos, source_pos, source_force):
    delta = target_pos[:, :, None] - source_pos[:, None, :]
    radius_sq = lax.optimization_barrier(jnp.sum(delta * delta, axis=0))
    shifted = radius_sq + blob_square
    inverse = 1.0 / (shifted * jnp.sqrt(shifted))
    along = lax.optimization_barrier(jnp.sum(delta * source_force[:, None, :], axis=0))
    direct = (radius_sq + 2.0 * blob_square) * inverse
    tensor = along * inverse
    return lax.optimization_barrier(jnp.sum(direct[None] * source_force[:, None, :] + tensor[None] * delta, axis=2))

def stokes_sum(target_pos, source_pos, source_force):
    count_target = target_pos.shape[1]
    count_source = source_pos.shape[1]
    target_rows = pick_block(count_target, 512)
    source_rows = pick_block(count_source, 2048)
    targets = target_pos.reshape(3, count_target // target_rows, target_rows).transpose(1, 0, 2)
    sources = source_pos.reshape(3, count_source // source_rows, source_rows).transpose(1, 0, 2)
    weights = source_force.reshape(3, count_source // source_rows, source_rows).transpose(1, 0, 2)

    def per_target(target_block):

        def add_block(running, blocks):
            return (running + stokes_block(target_block, blocks[0], blocks[1]), None)
        total, _ = lax.scan(add_block, jnp.zeros((3, target_rows), jnp.float32), (sources, weights))
        return total
    result = lax.map(per_target, targets)
    return result.transpose(1, 0, 2).reshape(3, count_target)

def cycle_weights():
    return jnp.concatenate([jnp.full((6,), 2.0 / 9.0, jnp.float32), jnp.full((6,), -1.0 / 18.0, jnp.float32)])

def membrane_force(edges, rest_length, moduli, rest_bend):
    nearest = edges[:, :6, :]
    stretch = lax.optimization_barrier(jnp.sum(nearest * nearest, axis=0)) / (rest_length * rest_length)
    tension = (stretch - 1.0) / (stretch + 1.0)
    surface = moduli[0] * lax.optimization_barrier(jnp.sum((tension / rest_length)[None] * nearest, axis=1))
    bending = lax.optimization_barrier(jnp.sum(cycle_weights()[None, :, None] * edges, axis=1)) - rest_bend
    return surface + moduli[1] * bending

def reference(positions, forces, neighbours, patch_owner, rest_length, moduli, rest_bend):
    devices = N_TGT * N_SRC
    total_nodes = positions.shape[1]
    owners = patch_owner[:, 0].reshape(devices, NODES_DEV)
    onehot = (owners[:, :, None] == jnp.arange(devices, dtype=jnp.int32)[None, None, :]).astype(jnp.int32)
    before = jnp.cumsum(onehot, axis=1) - onehot
    rank = lax.optimization_barrier(jnp.sum(before * onehot, axis=2))
    column = (owners * (devices * CAP) + jnp.arange(devices, dtype=jnp.int32)[:, None] * CAP + rank).reshape(total_nodes)
    node_length = rest_length[:, column]
    node_moduli = moduli[:, column]
    node_bend = rest_bend[:, column]
    base = jnp.arange(total_nodes, dtype=jnp.int32) // NODES_DEV * NODES_DEV
    stencil = neighbours + base[None, :]
    scale = 1.0 / math.sqrt(total_nodes)
    current = positions
    load = forces
    for update in range(STEPS):
        velocity = stokes_sum(current, current, load) * scale
        current = current + time_step * velocity
        edges = current[:, stencil] - current[:, None, :]
        load = membrane_force(edges, node_length, node_moduli, node_bend)
    velocity = stokes_sum(current, current, load) * scale
    return (current, velocity)
```

```python
import functools
import math

import jax
import jax.numpy as jnp
from jax import lax
from jax.experimental import pallas as pl
from jax.experimental.pallas import tpu as pltpu
from jax.sharding import PartitionSpec as P

F32, BF16 = jnp.float32, jnp.bfloat16
MESH = pl.DeviceIdType.MESH
STEPS = 3
EPS = 0.0025
TIME_STEP = 0.5
ROWS = 32
GROUP = 8
FIELDS = 12


def split3(v):
    high = v.astype(BF16).astype(F32)
    rest = v - high
    middle = rest.astype(BF16).astype(F32)
    return [high.astype(BF16), middle.astype(BF16), (rest - middle).astype(BF16)]


def dot(a, b, dims):
    return lax.dot_general(a, b, (dims, ((), ())), preferred_element_type=F32)


def kernel(n_src, devices, nodes, capacity, scale, pos_ref, frc_ref, nbr_ref, own_ref, par_ref, x_out, v_out,
           buf, blk, par_buf, par_own, prm, xb, acc, send_sem, recv_sem, par_send, par_recv):
    me = lax.axis_index("tgt") * n_src + lax.axis_index("src")
    groups = devices // GROUP

    def coords(k):
        t = lax.rem(me + k, devices)
        return (lax.div(t, n_src), lax.rem(t, n_src))

    barrier = pltpu.get_barrier_semaphore()

    @pl.loop(1, devices)
    def _(k):
        pl.semaphore_signal(barrier, inc=1, device_id=coords(k), device_id_type=MESH)

    zero_row = jnp.zeros((2, nodes), F32)
    blk[0] = jnp.concatenate([pos_ref[...], frc_ref[...], zero_row], axis=0)
    pl.semaphore_wait(barrier, devices - 1)

    def send_block(e):
        @pl.loop(1, devices)
        def _(k):
            pltpu.make_async_remote_copy(
                src_ref=blk.at[e], dst_ref=buf.at[e, k],
                send_sem=send_sem.at[e], recv_sem=recv_sem.at[e, lax.div(k, GROUP)],
                device_id=coords(k), device_id_type=MESH,
            ).start()

    def velocity(e):
        own = blk[e]
        buf[e, 0] = own
        parts = jnp.concatenate([p.astype(F32) for p in split3(own)], axis=0).astype(BF16)
        row = lax.broadcasted_iota(jnp.int32, (24, 128), 0)
        for c in range(3):
            pick = ((row % 8) == c).astype(F32).astype(BF16)
            xb[c] = dot(parts, pick, ((0,), (0,)))
        acc[...] = jnp.zeros_like(acc)

        @pl.loop(0, groups)
        def _(g):
            @pl.when(g == 0)
            def _():
                w = buf.at[e, pl.ds(1, GROUP - 1)]
                pltpu.make_async_remote_copy(w, w, send_sem.at[e], recv_sem.at[e, 0], device_id=coords(1), device_id_type=MESH).wait_recv()

            @pl.when(g > 0)
            def _():
                w = buf.at[e, pl.ds(g * GROUP, GROUP)]
                pltpu.make_async_remote_copy(w, w, send_sem.at[e], recv_sem.at[e, g], device_id=coords(1), device_id_type=MESH).wait_recv()

            @pl.loop(0, nodes // ROWS)
            def _(i):
                rows = pl.ds(pl.multiple_of(i * ROWS, ROWS), ROWS)
                x = [xb[c, rows, :] for c in range(3)]

                def step(j, total):
                    total = list(total)
                    for h in range(nodes // 128):
                        s = [buf[e, g * GROUP + j, c:c + 1, h * 128:(h + 1) * 128] for c in range(6)]
                        d = [x[c] - s[c] for c in range(3)]
                        q = d[0] * d[0] + (d[1] * d[1] + (d[2] * d[2] + EPS))
                        w = lax.rsqrt(q)
                        w3 = w * w * w
                        direct = w + EPS * w3
                        along = (d[0] * s[3] + d[1] * s[4] + d[2] * s[5]) * w3
                        for c in range(3):
                            total[c] = total[c] + (direct * s[3 + c] + along * d[c])
                    return tuple(total)

                total = lax.fori_loop(0, GROUP, step, tuple(acc[c, rows, :] for c in range(3)), unroll=2)
                for c in range(3):
                    acc[c, rows, :] = total[c]

        ones = jnp.ones((8, 128), BF16)
        out = []
        for c in range(3):
            h, m, l = split3(acc[c])
            out.append((dot(ones, h, ((1,), (1,))) + dot(ones, m, ((1,), (1,))) + dot(ones, l, ((1,), (1,))))[0:1])
        return jnp.concatenate(out, axis=0) * scale

    def take_params():
        w = par_buf.at[pl.ds(0, devices - 1)]
        pltpu.make_async_remote_copy(w, w, par_send, par_recv, device_id=coords(1), device_id_type=MESH).wait_recv()
        par_buf[me] = par_own[...]
        table = par_buf[...].reshape(devices, 128)
        owner = own_ref[...]
        hot = (lax.broadcasted_iota(jnp.int32, (devices, nodes), 0) == owner).astype(F32)
        hot16 = hot.astype(BF16)
        earlier = (lax.broadcasted_iota(jnp.int32, (nodes, nodes), 0) < lax.broadcasted_iota(jnp.int32, (nodes, nodes), 1))
        before = dot(hot16, earlier.astype(F32).astype(BF16), ((1,), (0,)))
        rank = jnp.sum(before * hot, axis=0, keepdims=True)
        rows = sum(dot(p, hot16, ((0,), (0,))) for p in split3(table))
        place = lax.broadcasted_iota(jnp.int32, (128, nodes), 0)
        base = rank.astype(jnp.int32) * FIELDS
        rows = jnp.where((place >= base) & (place < base + FIELDS), rows, 0.0)
        fold = ((lax.broadcasted_iota(jnp.int32, (16, 128), 1) % FIELDS) == lax.broadcasted_iota(jnp.int32, (16, 128), 0))
        fold = fold.astype(F32).astype(BF16)
        prm[...] = sum(dot(fold, p, ((1,), (0,))) for p in split3(rows))

    def membrane(x):
        length, modulus, bend = prm[0:6], prm[6:8], prm[8:11]
        index = nbr_ref[...]
        index = jnp.concatenate([index, index[:4]], axis=0)
        edges = []
        for c in range(3):
            halves = []
            for h in range(nodes // 128):
                where = index[:, h * 128:(h + 1) * 128]
                low = lax.rem(where, 128)
                got = None
                for s in range(nodes // 128):
                    pool = jnp.broadcast_to(x[c:c + 1, s * 128:(s + 1) * 128], (16, 128))
                    one = jnp.concatenate([jnp.take_along_axis(pool[k:k + 8], low[k:k + 8], axis=1) for k in (0, 8)], axis=0)
                    got = one if got is None else jnp.where(where >= s * 128, one, got)
                halves.append(got)
            edges.append(jnp.concatenate(halves, axis=1)[:12] - x[c:c + 1])
        square = edges[0][:6] ** 2 + edges[1][:6] ** 2 + edges[2][:6] ** 2
        stretch = square / (length * length)
        tension = (stretch - 1.0) / (stretch + 1.0) / length
        out = []
        for c in range(3):
            surface = modulus[0:1] * jnp.sum(tension * edges[c][:6], axis=0, keepdims=True)
            near = jnp.sum(edges[c][:6], axis=0, keepdims=True) * (2.0 / 9.0)
            far = jnp.sum(edges[c][6:], axis=0, keepdims=True) * (1.0 / 18.0)
            out.append(surface + modulus[1:2] * (near - far - bend[c:c + 1]))
        return jnp.concatenate(out, axis=0)

    send_block(0)
    par_own[...] = par_ref[me]

    @pl.loop(1, devices)
    def _(k):
        t = lax.rem(me + k, devices)
        pltpu.make_async_remote_copy(
            src_ref=par_ref.at[t], dst_ref=par_buf.at[me], send_sem=par_send, recv_sem=par_recv,
            device_id=coords(k), device_id_type=MESH,
        ).start()

    @pl.loop(0, STEPS)
    def _(e):
        u = velocity(e)
        x = blk[e][0:3] + TIME_STEP * u

        @pl.when(e == 0)
        def _():
            take_params()

        blk[e + 1] = jnp.concatenate([x, membrane(x), zero_row], axis=0)
        send_block(e + 1)

    x_out[...] = blk[STEPS][0:3]
    v_out[...] = velocity(STEPS)
    for e in range(STEPS + 1):
        w = buf.at[e, pl.ds(1, devices - 1)]
        pltpu.make_async_remote_copy(w, w, send_sem.at[e], recv_sem.at[e, 0], device_id=coords(1), device_id_type=MESH).wait_send()
    w = par_buf.at[pl.ds(0, devices - 1)]
    pltpu.make_async_remote_copy(w, w, par_send, par_recv, device_id=coords(1), device_id_type=MESH).wait_send()


def solution(mesh):
    n_tgt, n_src = mesh.shape["tgt"], mesh.shape["src"]
    devices = n_tgt * n_src

    def body(positions, forces, neighbours, patch_owner, rest_length, moduli, rest_bend):
        nodes = positions.shape[1]
        capacity = rest_length.shape[1] // devices
        fields = jnp.concatenate([rest_length, moduli, rest_bend, jnp.zeros_like(moduli[:1])], axis=0)
        table = fields.reshape(FIELDS, devices, capacity).transpose(1, 2, 0).reshape(devices, 1, capacity * FIELDS)
        table = jnp.pad(table, ((0, 0), (0, 0), (0, 128 - capacity * FIELDS)))
        vmem = pl.BlockSpec(memory_space=pltpu.VMEM)
        return pl.pallas_call(
            functools.partial(kernel, n_src, devices, nodes, capacity, 1.0 / math.sqrt(nodes * devices)),
            name="stokes",
            out_shape=(jax.ShapeDtypeStruct((3, nodes), F32), jax.ShapeDtypeStruct((3, nodes), F32)),
            in_specs=[vmem] * 5,
            out_specs=(vmem, vmem),
            scratch_shapes=[
                pltpu.VMEM((STEPS + 1, devices, 8, nodes), F32),
                pltpu.VMEM((STEPS + 1, 8, nodes), F32),
                pltpu.VMEM((devices, 1, 128), F32),
                pltpu.VMEM((1, 128), F32),
                pltpu.VMEM((16, nodes), F32),
                pltpu.VMEM((3, nodes, 128), F32),
                pltpu.VMEM((3, nodes, 128), F32),
                pltpu.SemaphoreType.DMA((STEPS + 1,)),
                pltpu.SemaphoreType.DMA((STEPS + 1, devices // GROUP)),
                pltpu.SemaphoreType.DMA,
                pltpu.SemaphoreType.DMA,
            ],
            compiler_params=pltpu.CompilerParams(collective_id=0, has_side_effects=True, vmem_limit_bytes=48 * 1024 * 1024),
        )(positions, forces, neighbours, patch_owner.reshape(1, nodes), table)

    cut = P(None, ("tgt", "src"))
    return jax.shard_map(
        body,
        mesh=mesh,
        in_specs=(cut, cut, cut, P(("tgt", "src"), None), cut, cut, cut),
        out_specs=(cut, cut),
        check_vma=False,
    )
```

```python
import functools
import math

import jax
import jax.numpy as jnp
from jax import lax
from jax.experimental import pallas as pl
from jax.experimental.pallas import tpu as pltpu
from jax.sharding import PartitionSpec as P

F32, BF16 = jnp.float32, jnp.bfloat16
MESH = pl.DeviceIdType.MESH
STEPS = 3
EPS = 0.0025
TIME_STEP = 0.5
ROWS = 16
GROUP = 8
FIELDS = 12


def split3(v):
    high = v.astype(BF16).astype(F32)
    rest = v - high
    middle = rest.astype(BF16).astype(F32)
    return [high.astype(BF16), middle.astype(BF16), (rest - middle).astype(BF16)]


def dot(a, b, dims):
    return lax.dot_general(a, b, (dims, ((), ())), preferred_element_type=F32)


def kernel(n_src, devices, nodes, capacity, scale, pos_ref, frc_ref, nbr_ref, own_ref, par_ref, x_out, v_out,
           buf, blk, ret, out, par_buf, par_own, prm, xb, lhs, prod, acc, near, send_sem, recv_sem, ret_send, ret_recv, par_send, par_recv):
    me = lax.axis_index("tgt") * n_src + lax.axis_index("src")
    half = devices // 2
    groups = half // GROUP

    def coords(k):
        t = lax.rem(me + k, devices)
        return (lax.div(t, n_src), lax.rem(t, n_src))

    barrier = pltpu.get_barrier_semaphore()

    @pl.loop(1, devices)
    def _(k):
        pl.semaphore_signal(barrier, inc=1, device_id=coords(k), device_id_type=MESH)

    def pack(x, f):
        return jnp.concatenate([x, f, jnp.sum(x * f, axis=0, keepdims=True), jnp.ones((1, nodes), F32)], axis=0)

    blk[0] = pack(pos_ref[...], frc_ref[...])
    pl.semaphore_wait(barrier, devices - 1)

    def send_block(e):
        @pl.loop(0, half)
        def _(k):
            pltpu.make_async_remote_copy(
                src_ref=blk.at[e], dst_ref=buf.at[e, k],
                send_sem=send_sem.at[e], recv_sem=recv_sem.at[e, lax.div(k, GROUP)],
                device_id=coords(k + 1), device_id_type=MESH,
            ).start()

    def wait_group(e, g):
        w = buf.at[e, pl.ds(g * GROUP, GROUP)]
        pltpu.make_async_remote_copy(w, w, send_sem.at[e], recv_sem.at[e, g], device_id=coords(1), device_id_type=MESH).wait_recv()

    def slot(s):
        g = lax.div(s, GROUP)
        g = jnp.where(g == 0, 0, jnp.where(g == groups - 1, 1, g + 1))
        return g * GROUP + lax.rem(s, GROUP), g

    def send_params(first, count):
        @pl.loop(first, first + count)
        def _(k):
            t = lax.rem(me + k, devices)

            @pl.when(k < devices)
            def _():
                pltpu.make_async_remote_copy(
                    src_ref=par_ref.at[t], dst_ref=par_buf.at[me], send_sem=par_send, recv_sem=par_recv,
                    device_id=coords(k), device_id_type=MESH,
                ).start()

    def velocity(e):
        own = blk[e]
        own_parts = split3(own)
        parts = jnp.concatenate([p.astype(F32) for p in own_parts], axis=0).astype(BF16)
        row = lax.broadcasted_iota(jnp.int32, (24, 128), 0)
        for c in range(3):
            pick = ((row % 8) == c).astype(F32).astype(BF16)
            xb[c] = dot(parts, pick, ((0,), (0,)))
        none = jnp.zeros((3, nodes), F32)
        one = jnp.ones((1, nodes), F32)
        fields = (jnp.concatenate([none, own[0:3], -one, one * 0.0], axis=0),
                  jnp.concatenate([-own[3:6], none, one * 0.0, own[6:7]], axis=0))
        for i, field in enumerate(fields):
            h, m, l = [p.astype(F32) for p in split3(field)]
            lhs[i * nodes:(i + 1) * nodes, :] = jnp.concatenate([h, h, m, m, h, l], axis=0).T.astype(BF16)
        acc[...] = jnp.zeros_like(acc)
        near[...] = jnp.zeros_like(near)

        def expand(g):
            h, m, l = [p.astype(F32) for p in split3(g)]
            return jnp.concatenate([h, m, h, m, l, h], axis=0).astype(BF16), jnp.concatenate([h, m], axis=0).astype(BF16)

        def products(g, p):
            prod[p] = dot(lhs[...], expand(g)[0], ((1,), (0,)))

        def pair(g, p, both):
            mine = expand(blk[e])[1]
            theirs = expand(g)[1]
            high, low = [], []
            back = [[None] * 3 for _ in range(nodes // 128)]
            for r in range(0, nodes, ROWS):
                rows = slice(r, r + ROWS)
                total = [acc[c, rows, :] for c in range(3)]
                highs, lows = [], []
                for h in range(nodes // 128):
                    cols = slice(h * 128, (h + 1) * 128)
                    d = [xb[c, rows, :] - g[c:c + 1, cols] for c in range(3)]
                    q = d[0] * d[0] + (d[1] * d[1] + (d[2] * d[2] + EPS))
                    w = lax.rsqrt(q)
                    w3 = w * w * w
                    direct = w + EPS * w3
                    t = prod[p, rows, cols] * w3
                    for c in range(3):
                        total[c] = total[c] + t * d[c]
                    if both:
                        t = prod[p, nodes + r:nodes + r + ROWS, cols] * w3
                        for c in range(3):
                            v = t * d[c]
                            for k in range(0, ROWS, 8):
                                back[h][c] = v[k:k + 8] if back[h][c] is None else back[h][c] + v[k:k + 8]
                    top = direct.astype(BF16)
                    highs.append(top)
                    lows.append((direct - top.astype(F32)).astype(BF16))
                for c in range(3):
                    acc[c, rows, :] = total[c]
                high.append(jnp.concatenate(highs, axis=1))
                low.append(jnp.concatenate(lows, axis=1))
            high, low = jnp.concatenate(high, axis=0), jnp.concatenate(low, axis=0)
            near[...] += dot(theirs, high, ((1,), (1,))) + dot(theirs, low, ((1,), (1,)))
            if not both:
                return None
            rev = dot(mine, high, ((1,), (0,))) + dot(mine, low, ((1,), (0,)))
            along = [jnp.concatenate([jnp.sum(b[c], axis=0, keepdims=True) for b in back], axis=1) for c in range(3)]
            return jnp.concatenate(along, axis=0) + rev[3:6] + rev[11:14]

        def give_back(s):
            k, _ = slot(s)

            @pl.when(k < half - 1)
            def _():
                pltpu.make_async_remote_copy(
                    src_ref=out.at[e, k], dst_ref=ret.at[e, k],
                    send_sem=ret_send.at[e], recv_sem=ret_recv.at[e],
                    device_id=coords(devices - 1 - k), device_id_type=MESH,
                ).start()

        wait_group(e, 0)
        products(buf[e, 0], 0)

        @pl.loop(0, half // 2)
        def _(m):
            s = m * 2

            @pl.when((lax.rem(m, GROUP // 2) == GROUP // 2 - 1) & (m < half // 2 - 1))
            def _():
                wait_group(e, slot(s + 2)[1])

            @pl.when(m > 0)
            def _():
                give_back(s - 2)
                give_back(s - 1)

            if e is not STEPS:
                @pl.when(e == 0)
                def _():
                    send_params(1 + m * 4, 4)

            k0, k1 = slot(s)[0], slot(s + 1)[0]
            k2 = slot(jnp.minimum(s + 2, half - 1))[0]
            products(buf[e, k1], 1)
            out[e, k0] = pair(buf[e, k0], 0, True)
            products(jnp.where(m < half // 2 - 1, buf[e, k2], blk[e]), 0)
            out[e, k1] = pair(buf[e, k1], 1, True)

        give_back(half - 2)
        give_back(half - 1)
        pair(blk[e], 0, False)

        ones = jnp.ones((8, 128), BF16)
        total = []
        for c in range(3):
            total.append(sum(dot(ones, p, ((1,), (1,))) for p in split3(acc[c]))[0:1])
        total = jnp.concatenate(total, axis=0) + near[3:6] + near[11:14]
        w = ret.at[e, pl.ds(0, half - 1)]
        pltpu.make_async_remote_copy(w, w, ret_send.at[e], ret_recv.at[e], device_id=coords(1), device_id_type=MESH).wait_recv()
        total = total + jnp.sum(ret[e, 0:half - 1], axis=0)
        return total * scale

    def take_params():
        w = par_buf.at[pl.ds(0, devices - 1)]
        pltpu.make_async_remote_copy(w, w, par_send, par_recv, device_id=coords(1), device_id_type=MESH).wait_recv()
        par_buf[me] = par_own[...]
        table = par_buf[...].reshape(devices, 128)
        owner = own_ref[...]
        hot = (lax.broadcasted_iota(jnp.int32, (devices, nodes), 0) == owner).astype(F32)
        hot16 = hot.astype(BF16)
        earlier = (lax.broadcasted_iota(jnp.int32, (nodes, nodes), 0) < lax.broadcasted_iota(jnp.int32, (nodes, nodes), 1))
        before = dot(hot16, earlier.astype(F32).astype(BF16), ((1,), (0,)))
        rank = jnp.sum(before * hot, axis=0, keepdims=True)
        rows = sum(dot(p, hot16, ((0,), (0,))) for p in split3(table))
        place = lax.broadcasted_iota(jnp.int32, (128, nodes), 0)
        base = rank.astype(jnp.int32) * FIELDS
        rows = jnp.where((place >= base) & (place < base + FIELDS), rows, 0.0)
        fold = ((lax.broadcasted_iota(jnp.int32, (16, 128), 1) % FIELDS) == lax.broadcasted_iota(jnp.int32, (16, 128), 0))
        fold = fold.astype(F32).astype(BF16)
        prm[...] = sum(dot(fold, p, ((1,), (0,))) for p in split3(rows))

    def membrane(x):
        length, modulus, bend = prm[0:6], prm[6:8], prm[8:11]
        index = nbr_ref[...]
        index = jnp.concatenate([index, index[:4]], axis=0)
        edges = []
        for c in range(3):
            halves = []
            for h in range(nodes // 128):
                where = index[:, h * 128:(h + 1) * 128]
                low = lax.rem(where, 128)
                got = None
                for s in range(nodes // 128):
                    pool = jnp.broadcast_to(x[c:c + 1, s * 128:(s + 1) * 128], (16, 128))
                    one = jnp.concatenate([jnp.take_along_axis(pool[k:k + 8], low[k:k + 8], axis=1) for k in (0, 8)], axis=0)
                    got = one if got is None else jnp.where(where >= s * 128, one, got)
                halves.append(got)
            edges.append(jnp.concatenate(halves, axis=1)[:12] - x[c:c + 1])
        square = edges[0][:6] ** 2 + edges[1][:6] ** 2 + edges[2][:6] ** 2
        stretch = square / (length * length)
        tension = (stretch - 1.0) / (stretch + 1.0) / length
        out = []
        for c in range(3):
            surface = modulus[0:1] * jnp.sum(tension * edges[c][:6], axis=0, keepdims=True)
            near = jnp.sum(edges[c][:6], axis=0, keepdims=True) * (2.0 / 9.0)
            far = jnp.sum(edges[c][6:], axis=0, keepdims=True) * (1.0 / 18.0)
            out.append(surface + modulus[1:2] * (near - far - bend[c:c + 1]))
        return jnp.concatenate(out, axis=0)

    send_block(0)
    par_own[...] = par_ref[me]

    @pl.loop(0, STEPS)
    def _(e):
        u = velocity(e)
        x = blk[e][0:3] + TIME_STEP * u

        @pl.when(e == 0)
        def _():
            take_params()

        blk[e + 1] = pack(x, membrane(x))
        send_block(e + 1)

    x_out[...] = blk[STEPS][0:3]
    v_out[...] = velocity(STEPS)
    for e in range(STEPS + 1):
        w = buf.at[e]
        pltpu.make_async_remote_copy(w, w, send_sem.at[e], recv_sem.at[e, 0], device_id=coords(1), device_id_type=MESH).wait_send()
        w = ret.at[e, pl.ds(0, half - 1)]
        pltpu.make_async_remote_copy(w, w, ret_send.at[e], ret_recv.at[e], device_id=coords(1), device_id_type=MESH).wait_send()
    w = par_buf.at[pl.ds(0, devices - 1)]
    pltpu.make_async_remote_copy(w, w, par_send, par_recv, device_id=coords(1), device_id_type=MESH).wait_send()


def solution(mesh):
    n_tgt, n_src = mesh.shape["tgt"], mesh.shape["src"]
    devices = n_tgt * n_src

    def body(positions, forces, neighbours, patch_owner, rest_length, moduli, rest_bend):
        nodes = positions.shape[1]
        capacity = rest_length.shape[1] // devices
        fields = jnp.concatenate([rest_length, moduli, rest_bend, jnp.zeros_like(moduli[:1])], axis=0)
        table = fields.reshape(FIELDS, devices, capacity).transpose(1, 2, 0).reshape(devices, 1, capacity * FIELDS)
        table = jnp.pad(table, ((0, 0), (0, 0), (0, 128 - capacity * FIELDS)))
        vmem = pl.BlockSpec(memory_space=pltpu.VMEM)
        return pl.pallas_call(
            functools.partial(kernel, n_src, devices, nodes, capacity, 1.0 / math.sqrt(nodes * devices)),
            name="stokes",
            out_shape=(jax.ShapeDtypeStruct((3, nodes), F32), jax.ShapeDtypeStruct((3, nodes), F32)),
            in_specs=[vmem] * 5,
            out_specs=(vmem, vmem),
            scratch_shapes=[
                pltpu.VMEM((STEPS + 1, devices // 2, 8, nodes), F32),
                pltpu.VMEM((STEPS + 1, 8, nodes), F32),
                pltpu.VMEM((STEPS + 1, devices // 2, 3, nodes), F32),
                pltpu.VMEM((STEPS + 1, devices // 2, 3, nodes), F32),
                pltpu.VMEM((devices, 1, 128), F32),
                pltpu.VMEM((1, 128), F32),
                pltpu.VMEM((16, nodes), F32),
                pltpu.VMEM((3, nodes, 128), F32),
                pltpu.VMEM((2 * nodes, 48), BF16),
                pltpu.VMEM((2, 2 * nodes, nodes), F32),
                pltpu.VMEM((3, nodes, 128), F32),
                pltpu.VMEM((16, nodes), F32),
                pltpu.SemaphoreType.DMA((STEPS + 1,)),
                pltpu.SemaphoreType.DMA((STEPS + 1, devices // 2 // GROUP)),
                pltpu.SemaphoreType.DMA((STEPS + 1,)),
                pltpu.SemaphoreType.DMA((STEPS + 1,)),
                pltpu.SemaphoreType.DMA,
                pltpu.SemaphoreType.DMA,
            ],
            compiler_params=pltpu.CompilerParams(collective_id=0, has_side_effects=True, vmem_limit_bytes=48 * 1024 * 1024),
        )(positions, forces, neighbours, patch_owner.reshape(1, nodes), table)

    cut = P(None, ("tgt", "src"))
    return jax.shard_map(
        body,
        mesh=mesh,
        in_specs=(cut, cut, cut, P(("tgt", "src"), None), cut, cut, cut),
        out_specs=(cut, cut),
        check_vma=False,
    )
```

```python
import functools
import math

import jax
import jax.numpy as jnp
from jax import lax
from jax.experimental import pallas as pl
from jax.experimental.pallas import tpu as pltpu
from jax.sharding import PartitionSpec as P

F32, BF16 = jnp.float32, jnp.bfloat16
MESH = pl.DeviceIdType.MESH
STEPS = 3
EPS = 0.0025
TIME_STEP = 0.5
ROWS = 16
GROUP = 4
NEAR = 8
FIELDS = 12


def split3(v):
    high = v.astype(BF16).astype(F32)
    rest = v - high
    middle = rest.astype(BF16).astype(F32)
    return [high.astype(BF16), middle.astype(BF16), (rest - middle).astype(BF16)]


def dot(a, b, dims):
    return lax.dot_general(a, b, (dims, ((), ())), preferred_element_type=F32)


def kernel(n_src, devices, nodes, capacity, scale, pos_ref, frc_ref, nbr_ref, own_ref, par_ref, x_out, v_out,
           buf, blk, ret, out, par_buf, par_own, prm, xb, lhs, prod, acc, near, send_sem, recv_sem, ret_send, ret_recv, par_send, par_recv):
    me = lax.axis_index("tgt") * n_src + lax.axis_index("src")
    half = devices // 2
    groups = half // GROUP

    shift = n_src.bit_length() - 1

    def coords(k):
        t = (me + k) & (devices - 1)
        return (t >> shift, t & (n_src - 1))

    barrier = pltpu.get_barrier_semaphore()

    def greet(k):
        pl.semaphore_signal(barrier, inc=1, device_id=coords(k), device_id_type=MESH)

    @pl.loop(0, devices // 8 - 1)
    def _(k):
        for i in range(1, 9):
            greet(k * 8 + i)

    for i in range(devices - 7, devices):
        greet(i)

    def pack(x, f):
        return jnp.concatenate([x, f, jnp.sum(x * f, axis=0, keepdims=True), jnp.ones((1, nodes), F32)], axis=0)

    blk[0] = pack(pos_ref[...], frc_ref[...])
    pl.semaphore_wait(barrier, devices - 1)

    span = (half - NEAR) // NEAR

    def offset(t):
        return NEAR + 1 + lax.rem(t, span) * NEAR + lax.div(t, span)


    def send_block(e):
        def send(s, k):
            pltpu.make_async_remote_copy(
                src_ref=blk.at[e], dst_ref=buf.at[e, s],
                send_sem=send_sem.at[e], recv_sem=recv_sem.at[e, s // GROUP],
                device_id=coords(k), device_id_type=MESH,
            ).start()

        for i in range(NEAR // 2):
            send(i, i + 1)

        @pl.loop(0, span)
        def _(b):
            for a in range(NEAR):
                send(b * NEAR + NEAR // 2 + a, offset(b * NEAR + a))

        for i in range(NEAR // 2):
            send(half - NEAR // 2 + i, NEAR // 2 + 1 + i)

    def wait_group(e, g):
        w = buf.at[e, pl.ds(g * GROUP, GROUP)]
        pltpu.make_async_remote_copy(w, w, send_sem.at[e], recv_sem.at[e, g], device_id=coords(1), device_id_type=MESH).wait_recv()

    def partner(s):
        far = offset(s - NEAR // 2)
        return jnp.where(s < NEAR // 2, s + 1, jnp.where(s >= half - NEAR // 2, s - half + NEAR + 1, far))

    def send_params(first, count):
        @pl.loop(first, first + count)
        def _(k):
            t = (me + k) & (devices - 1)

            @pl.when(k < devices)
            def _():
                pltpu.make_async_remote_copy(
                    src_ref=par_ref.at[t], dst_ref=par_buf.at[me], send_sem=par_send, recv_sem=par_recv,
                    device_id=coords(k), device_id_type=MESH,
                ).start()

    def velocity(e):
        own = blk[e]
        own_parts = split3(own)
        parts = jnp.concatenate([p.astype(F32) for p in own_parts], axis=0).astype(BF16)
        row = lax.broadcasted_iota(jnp.int32, (24, 128), 0)
        for c in range(3):
            pick = ((row % 8) == c).astype(F32).astype(BF16)
            xb[c] = dot(parts, pick, ((0,), (0,)))
        none = jnp.zeros((3, nodes), F32)
        one = jnp.ones((1, nodes), F32)
        fields = (jnp.concatenate([none, own[0:3], -one, one * 0.0], axis=0),
                  jnp.concatenate([-own[3:6], none, one * 0.0, own[6:7]], axis=0))
        for i, field in enumerate(fields):
            h, m, l = [p.astype(F32) for p in split3(field)]
            lhs[i * nodes:(i + 1) * nodes, :] = jnp.concatenate([h, h, m, m, h, l], axis=0).T.astype(BF16)
        acc[...] = jnp.zeros_like(acc)
        near[...] = jnp.zeros_like(near)

        def expand(g):
            h, m, l = [p.astype(F32) for p in split3(g)]
            return jnp.concatenate([h, m, h, m, l, h], axis=0).astype(BF16), jnp.concatenate([h, m], axis=0).astype(BF16)

        def products(g, p):
            prod[p] = dot(lhs[...], expand(g)[0], ((1,), (0,)))

        def pair(g, p, both):
            mine = expand(blk[e])[1]
            theirs = expand(g)[1]
            high, low = [], []
            back = [[None] * 3 for _ in range(nodes // 128)]
            for r in range(0, nodes, ROWS):
                rows = slice(r, r + ROWS)
                total = [acc[c, rows, :] for c in range(3)]
                highs, lows = [], []
                for h in range(nodes // 128):
                    cols = slice(h * 128, (h + 1) * 128)
                    d = [xb[c, rows, :] - g[c:c + 1, cols] for c in range(3)]
                    q = d[0] * d[0] + (d[1] * d[1] + (d[2] * d[2] + EPS))
                    w = lax.rsqrt(q)
                    w3 = w * w * w
                    direct = w + EPS * w3
                    t = prod[p, rows, cols] * w3
                    for c in range(3):
                        total[c] = total[c] + t * d[c]
                    if both:
                        t = prod[p, nodes + r:nodes + r + ROWS, cols] * w3
                        for c in range(3):
                            v = t * d[c]
                            for k in range(0, ROWS, 8):
                                back[h][c] = v[k:k + 8] if back[h][c] is None else back[h][c] + v[k:k + 8]
                    top = direct.astype(BF16)
                    highs.append(top)
                    lows.append((direct - top.astype(F32)).astype(BF16))
                for c in range(3):
                    acc[c, rows, :] = total[c]
                high.append(jnp.concatenate(highs, axis=1))
                low.append(jnp.concatenate(lows, axis=1))
            high, low = jnp.concatenate(high, axis=0), jnp.concatenate(low, axis=0)
            near[...] += dot(theirs, high, ((1,), (1,))) + dot(theirs, low, ((1,), (1,)))
            if not both:
                return None
            rev = dot(mine, high, ((1,), (0,))) + dot(mine, low, ((1,), (0,)))
            along = [jnp.concatenate([jnp.sum(b[c], axis=0, keepdims=True) for b in back], axis=1) for c in range(3)]
            return jnp.concatenate(along, axis=0) + rev[3:6] + rev[11:14]

        def give_back(s):
            k = partner(s)

            @pl.when(k < half)
            def _():
                pltpu.make_async_remote_copy(
                    src_ref=out.at[e, s], dst_ref=ret.at[e, k - 1],
                    send_sem=ret_send.at[e], recv_sem=ret_recv.at[e],
                    device_id=coords(devices - k), device_id_type=MESH,
                ).start()

        wait_group(e, 0)
        products(buf[e, 0], 0)

        @pl.loop(0, half // 2)
        def _(m):
            s = m * 2

            @pl.when((lax.rem(m, GROUP // 2) == GROUP // 2 - 1) & (m < half // 2 - 1))
            def _():
                wait_group(e, lax.div(s, GROUP) + 1)

            @pl.when(m > 0)
            def _():
                give_back(s - 2)
                give_back(s - 1)

            if e is not STEPS:
                @pl.when(e == 0)
                def _():
                    send_params(1 + m * 4, 4)

            products(buf[e, s + 1], 1)
            out[e, s] = pair(buf[e, s], 0, True)
            products(jnp.where(m < half // 2 - 1, buf[e, jnp.minimum(s + 2, half - 1)], blk[e]), 0)
            out[e, s + 1] = pair(buf[e, s + 1], 1, True)

        give_back(half - 2)
        give_back(half - 1)
        pair(blk[e], 0, False)

        ones = jnp.ones((8, 128), BF16)
        total = []
        for c in range(3):
            total.append(sum(dot(ones, p, ((1,), (1,))) for p in split3(acc[c]))[0:1])
        total = jnp.concatenate(total, axis=0) + near[3:6] + near[11:14]
        w = ret.at[e, pl.ds(0, half - 1)]
        pltpu.make_async_remote_copy(w, w, ret_send.at[e], ret_recv.at[e], device_id=coords(1), device_id_type=MESH).wait_recv()
        total = total + jnp.sum(ret[e, 0:half - 1], axis=0)
        return total * scale

    def take_params():
        w = par_buf.at[pl.ds(0, devices - 1)]
        pltpu.make_async_remote_copy(w, w, par_send, par_recv, device_id=coords(1), device_id_type=MESH).wait_recv()
        par_buf[me] = par_own[...]
        table = par_buf[...].reshape(devices, 128)
        owner = own_ref[...]
        hot = (lax.broadcasted_iota(jnp.int32, (devices, nodes), 0) == owner).astype(F32)
        hot16 = hot.astype(BF16)
        earlier = (lax.broadcasted_iota(jnp.int32, (nodes, nodes), 0) < lax.broadcasted_iota(jnp.int32, (nodes, nodes), 1))
        before = dot(hot16, earlier.astype(F32).astype(BF16), ((1,), (0,)))
        rank = jnp.sum(before * hot, axis=0, keepdims=True)
        rows = sum(dot(p, hot16, ((0,), (0,))) for p in split3(table))
        place = lax.broadcasted_iota(jnp.int32, (128, nodes), 0)
        base = rank.astype(jnp.int32) * FIELDS
        rows = jnp.where((place >= base) & (place < base + FIELDS), rows, 0.0)
        fold = ((lax.broadcasted_iota(jnp.int32, (16, 128), 1) % FIELDS) == lax.broadcasted_iota(jnp.int32, (16, 128), 0))
        fold = fold.astype(F32).astype(BF16)
        prm[...] = sum(dot(fold, p, ((1,), (0,))) for p in split3(rows))

    def membrane(x):
        length, modulus, bend = prm[0:6], prm[6:8], prm[8:11]
        index = nbr_ref[...]
        index = jnp.concatenate([index, index[:4]], axis=0)
        edges = []
        for c in range(3):
            halves = []
            for h in range(nodes // 128):
                where = index[:, h * 128:(h + 1) * 128]
                low = lax.rem(where, 128)
                got = None
                for s in range(nodes // 128):
                    pool = jnp.broadcast_to(x[c:c + 1, s * 128:(s + 1) * 128], (16, 128))
                    one = jnp.concatenate([jnp.take_along_axis(pool[k:k + 8], low[k:k + 8], axis=1) for k in (0, 8)], axis=0)
                    got = one if got is None else jnp.where(where >= s * 128, one, got)
                halves.append(got)
            edges.append(jnp.concatenate(halves, axis=1)[:12] - x[c:c + 1])
        square = edges[0][:6] ** 2 + edges[1][:6] ** 2 + edges[2][:6] ** 2
        stretch = square / (length * length)
        tension = (stretch - 1.0) / (stretch + 1.0) / length
        out = []
        for c in range(3):
            surface = modulus[0:1] * jnp.sum(tension * edges[c][:6], axis=0, keepdims=True)
            near = jnp.sum(edges[c][:6], axis=0, keepdims=True) * (2.0 / 9.0)
            far = jnp.sum(edges[c][6:], axis=0, keepdims=True) * (1.0 / 18.0)
            out.append(surface + modulus[1:2] * (near - far - bend[c:c + 1]))
        return jnp.concatenate(out, axis=0)

    send_block(0)
    par_own[...] = par_ref[me]

    @pl.loop(0, STEPS)
    def _(e):
        u = velocity(e)
        x = blk[e][0:3] + TIME_STEP * u

        @pl.when(e == 0)
        def _():
            take_params()

        blk[e + 1] = pack(x, membrane(x))
        send_block(e + 1)

    x_out[...] = blk[STEPS][0:3]
    v_out[...] = velocity(STEPS)
    for e in range(STEPS + 1):
        w = buf.at[e]
        pltpu.make_async_remote_copy(w, w, send_sem.at[e], recv_sem.at[e, 0], device_id=coords(1), device_id_type=MESH).wait_send()
        w = ret.at[e, pl.ds(0, half - 1)]
        pltpu.make_async_remote_copy(w, w, ret_send.at[e], ret_recv.at[e], device_id=coords(1), device_id_type=MESH).wait_send()
    w = par_buf.at[pl.ds(0, devices - 1)]
    pltpu.make_async_remote_copy(w, w, par_send, par_recv, device_id=coords(1), device_id_type=MESH).wait_send()


def solution(mesh):
    n_tgt, n_src = mesh.shape["tgt"], mesh.shape["src"]
    devices = n_tgt * n_src

    def body(positions, forces, neighbours, patch_owner, rest_length, moduli, rest_bend):
        nodes = positions.shape[1]
        capacity = rest_length.shape[1] // devices
        fields = jnp.concatenate([rest_length, moduli, rest_bend, jnp.zeros_like(moduli[:1])], axis=0)
        table = fields.reshape(FIELDS, devices, capacity).transpose(1, 2, 0).reshape(devices, 1, capacity * FIELDS)
        table = jnp.pad(table, ((0, 0), (0, 0), (0, 128 - capacity * FIELDS)))
        vmem = pl.BlockSpec(memory_space=pltpu.VMEM)
        return pl.pallas_call(
            functools.partial(kernel, n_src, devices, nodes, capacity, 1.0 / math.sqrt(nodes * devices)),
            name="stokes",
            out_shape=(jax.ShapeDtypeStruct((3, nodes), F32), jax.ShapeDtypeStruct((3, nodes), F32)),
            in_specs=[vmem] * 5,
            out_specs=(vmem, vmem),
            scratch_shapes=[
                pltpu.VMEM((STEPS + 1, devices // 2, 8, nodes), F32),
                pltpu.VMEM((STEPS + 1, 8, nodes), F32),
                pltpu.VMEM((STEPS + 1, devices // 2, 3, nodes), F32),
                pltpu.VMEM((STEPS + 1, devices // 2, 3, nodes), F32),
                pltpu.VMEM((devices, 1, 128), F32),
                pltpu.VMEM((1, 128), F32),
                pltpu.VMEM((16, nodes), F32),
                pltpu.VMEM((3, nodes, 128), F32),
                pltpu.VMEM((2 * nodes, 48), BF16),
                pltpu.VMEM((2, 2 * nodes, nodes), F32),
                pltpu.VMEM((3, nodes, 128), F32),
                pltpu.VMEM((16, nodes), F32),
                pltpu.SemaphoreType.DMA((STEPS + 1,)),
                pltpu.SemaphoreType.DMA((STEPS + 1, devices // 2 // GROUP)),
                pltpu.SemaphoreType.DMA((STEPS + 1,)),
                pltpu.SemaphoreType.DMA((STEPS + 1,)),
                pltpu.SemaphoreType.DMA,
                pltpu.SemaphoreType.DMA,
            ],
            compiler_params=pltpu.CompilerParams(collective_id=0, has_side_effects=True, vmem_limit_bytes=48 * 1024 * 1024),
        )(positions, forces, neighbours, patch_owner.reshape(1, nodes), table)

    cut = P(None, ("tgt", "src"))
    return jax.shard_map(
        body,
        mesh=mesh,
        in_specs=(cut, cut, cut, P(("tgt", "src"), None), cut, cut, cut),
        out_specs=(cut, cut),
        check_vma=False,
    )
```

```python
import functools
import math

import jax
import jax.numpy as jnp
from jax import lax
from jax.experimental import pallas as pl
from jax.experimental.pallas import tpu as pltpu
from jax.sharding import PartitionSpec as P

F32, BF16 = jnp.float32, jnp.bfloat16
MESH = pl.DeviceIdType.MESH
STEPS = 3
EPS = 0.0025
TIME_STEP = 0.5
ROWS = 16
NEAR = 4
AHEAD = 16
FIELDS = 12


def split3(v):
    high = v.astype(BF16).astype(F32)
    rest = v - high
    middle = rest.astype(BF16).astype(F32)
    return [high.astype(BF16), middle.astype(BF16), (rest - middle).astype(BF16)]


def dot(a, b, dims):
    return lax.dot_general(a, b, (dims, ((), ())), preferred_element_type=F32)


def kernel(n_src, devices, nodes, capacity, scale, pos_ref, frc_ref, nbr_ref, own_ref, par_ref, x_out, v_out,
           buf, blk, ret, out, par_buf, par_own, prm, xb, lhs, prod, acc, near, send_sem, recv_sem, ret_send, ret_recv, par_send, par_recv):
    me = lax.axis_index("tgt") * n_src + lax.axis_index("src")
    half = devices // 2

    shift = n_src.bit_length() - 1

    def coords(k):
        t = (me + k) & (devices - 1)
        return (t >> shift, t & (n_src - 1))

    barrier = pltpu.get_barrier_semaphore()

    def greet(k):
        pl.semaphore_signal(barrier, inc=1, device_id=coords(k), device_id_type=MESH)

    @pl.loop(0, devices // 8 - 1)
    def _(k):
        for i in range(1, 9):
            greet(k * 8 + i)

    for i in range(devices - 7, devices):
        greet(i)

    def pack(x, f):
        return jnp.concatenate([x, f, jnp.sum(x * f, axis=0, keepdims=True), jnp.ones((1, nodes), F32)], axis=0)

    blk[0] = pack(pos_ref[...], frc_ref[...])
    pl.semaphore_wait(barrier, devices - 1)

    def partner(s):
        t = s - NEAR - 1
        far = 2 * NEAR + 1 + (t & 7) * ((half - 2 * NEAR) // 8) + (t >> 3)
        near_by = jnp.where(s == half, half, s - half + 2 * NEAR + 1)
        return jnp.where(s <= NEAR, s, jnp.where(s >= half - NEAR, near_by, far))

    def send_block(e, s):
        pltpu.make_async_remote_copy(
            src_ref=blk.at[e, pl.ds(0, 6)], dst_ref=buf.at[e, s, pl.ds(0, 6)],
            send_sem=send_sem.at[e], recv_sem=recv_sem.at[e, (s - 1) >> 1],
            device_id=coords(partner(s)), device_id_type=MESH,
        ).start()

    def send_first(e):
        for s in range(1, AHEAD + 1):
            send_block(e, jnp.int32(s))

    def wait_pair(e, m):
        w = buf.at[e, pl.ds(2 * m + 1, 2), pl.ds(0, 6)]
        pltpu.make_async_remote_copy(w, w, send_sem.at[e], recv_sem.at[e, m], device_id=coords(1), device_id_type=MESH).wait_recv()

    def send_params(first, count):
        @pl.loop(first, first + count)
        def _(k):
            t = (me + k) & (devices - 1)

            @pl.when(k < devices)
            def _():
                pltpu.make_async_remote_copy(
                    src_ref=par_ref.at[t], dst_ref=par_buf.at[me], send_sem=par_send, recv_sem=par_recv,
                    device_id=coords(k), device_id_type=MESH,
                ).start()

    def velocity(e):
        own = blk[e]
        buf[e, 0] = own
        own_parts = split3(own)
        parts = jnp.concatenate([p.astype(F32) for p in own_parts], axis=0).astype(BF16)
        row = lax.broadcasted_iota(jnp.int32, (24, 128), 0)
        for c in range(3):
            pick = ((row % 8) == c).astype(F32).astype(BF16)
            xb[c] = dot(parts, pick, ((0,), (0,)))
        none = jnp.zeros((3, nodes), F32)
        one = jnp.ones((1, nodes), F32)
        fields = (jnp.concatenate([none, own[0:3], -one, one * 0.0], axis=0),
                  jnp.concatenate([-own[3:6], none, one * 0.0, own[6:7]], axis=0))
        for i, field in enumerate(fields):
            h, m, l = [p.astype(F32) for p in split3(field)]
            lhs[i * nodes:(i + 1) * nodes, :] = jnp.concatenate([h, h, m, m, h, l], axis=0).T.astype(BF16)
        acc[...] = jnp.zeros_like(acc)
        near[...] = jnp.zeros_like(near)

        def expand(g):
            return [p.astype(F32) for p in split3(pack(g[0:3], g[3:6]))]

        def products(g, p):
            h, m, l = expand(g)
            prod[p] = dot(lhs[...], jnp.concatenate([h, m, h, m, l, h], axis=0).astype(BF16), ((1,), (0,)))

        def two(g):
            h, m, _ = expand(g)
            return jnp.concatenate([h, m], axis=0).astype(BF16)

        def pair(g, p, both):
            mine = two(blk[e])
            theirs = two(g)
            high, low = [], []
            back = [[None] * 3 for _ in range(nodes // 128)]
            for r in range(0, nodes, ROWS):
                rows = slice(r, r + ROWS)
                total = [acc[c, rows, :] for c in range(3)]
                highs, lows = [], []
                for h in range(nodes // 128):
                    cols = slice(h * 128, (h + 1) * 128)
                    d = [xb[c, rows, :] - g[c:c + 1, cols] for c in range(3)]
                    q = d[0] * d[0] + (d[1] * d[1] + (d[2] * d[2] + EPS))
                    w = lax.rsqrt(q)
                    w3 = w * w * w
                    direct = w + EPS * w3
                    t = prod[p, rows, cols] * w3
                    for c in range(3):
                        total[c] = total[c] + t * d[c]
                    if both:
                        t = prod[p, nodes + r:nodes + r + ROWS, cols] * w3
                        for c in range(3):
                            v = t * d[c]
                            for k in range(0, ROWS, 8):
                                back[h][c] = v[k:k + 8] if back[h][c] is None else back[h][c] + v[k:k + 8]
                    top = direct.astype(BF16)
                    highs.append(top)
                    lows.append((direct - top.astype(F32)).astype(BF16))
                for c in range(3):
                    acc[c, rows, :] = total[c]
                high.append(jnp.concatenate(highs, axis=1))
                low.append(jnp.concatenate(lows, axis=1))
            high, low = jnp.concatenate(high, axis=0), jnp.concatenate(low, axis=0)
            near[...] += dot(theirs, high, ((1,), (1,))) + dot(theirs, low, ((1,), (1,)))
            if not both:
                return None
            rev = dot(mine, high, ((1,), (0,))) + dot(mine, low, ((1,), (0,)))
            along = [jnp.concatenate([jnp.sum(b[c], axis=0, keepdims=True) for b in back], axis=1) for c in range(3)]
            return jnp.concatenate(along, axis=0) + rev[3:6] + rev[11:14]

        def give_back(s):
            k = partner(s)

            @pl.when((s > 0) & (s < half))
            def _():
                pltpu.make_async_remote_copy(
                    src_ref=out.at[e, s], dst_ref=ret.at[e, k - 1],
                    send_sem=ret_send.at[e], recv_sem=ret_recv.at[e],
                    device_id=coords(devices - k), device_id_type=MESH,
                ).start()

        products(own, 0)

        @pl.loop(0, half // 2)
        def _(m):
            s = m * 2

            @pl.when(m < (half - AHEAD) // 2)
            def _():
                send_block(e, AHEAD + 1 + s)
                send_block(e, AHEAD + 2 + s)

            if e is not STEPS:
                @pl.when(e == 0)
                def _():
                    send_params(1 + m * 4, 4)

            @pl.when(m > 0)
            def _():
                give_back(s - 2)
                give_back(s - 1)

            wait_pair(e, m)
            products(buf[e, s + 1, 0:6], 1)
            out[e, s] = pair(buf[e, s, 0:6], 0, True)
            products(buf[e, s + 2, 0:6], 0)
            out[e, s + 1] = pair(buf[e, s + 1, 0:6], 1, True)

        give_back(jnp.int32(half - 2))
        give_back(jnp.int32(half - 1))
        pair(buf[e, half, 0:6], 0, False)

        ones = jnp.ones((8, 128), BF16)
        total = []
        for c in range(3):
            total.append(sum(dot(ones, p, ((1,), (1,))) for p in split3(acc[c]))[0:1])
        total = jnp.concatenate(total, axis=0) + near[3:6] + near[11:14]
        w = ret.at[e, pl.ds(0, half - 1)]
        pltpu.make_async_remote_copy(w, w, ret_send.at[e], ret_recv.at[e], device_id=coords(1), device_id_type=MESH).wait_recv()
        total = total + jnp.sum(ret[e, 0:half - 1], axis=0)
        return total * scale

    def take_params():
        w = par_buf.at[pl.ds(0, devices - 1)]
        pltpu.make_async_remote_copy(w, w, par_send, par_recv, device_id=coords(1), device_id_type=MESH).wait_recv()
        par_buf[me] = par_own[...]
        table = par_buf[...].reshape(devices, 128)
        owner = own_ref[...]
        hot = (lax.broadcasted_iota(jnp.int32, (devices, nodes), 0) == owner).astype(F32)
        hot16 = hot.astype(BF16)
        earlier = (lax.broadcasted_iota(jnp.int32, (nodes, nodes), 0) < lax.broadcasted_iota(jnp.int32, (nodes, nodes), 1))
        before = dot(hot16, earlier.astype(F32).astype(BF16), ((1,), (0,)))
        rank = jnp.sum(before * hot, axis=0, keepdims=True)
        rows = sum(dot(p, hot16, ((0,), (0,))) for p in split3(table))
        place = lax.broadcasted_iota(jnp.int32, (128, nodes), 0)
        base = rank.astype(jnp.int32) * FIELDS
        rows = jnp.where((place >= base) & (place < base + FIELDS), rows, 0.0)
        fold = ((lax.broadcasted_iota(jnp.int32, (16, 128), 1) % FIELDS) == lax.broadcasted_iota(jnp.int32, (16, 128), 0))
        fold = fold.astype(F32).astype(BF16)
        prm[...] = sum(dot(fold, p, ((1,), (0,))) for p in split3(rows))

    def membrane(x):
        length, modulus, bend = prm[0:6], prm[6:8], prm[8:11]
        index = nbr_ref[...]
        index = jnp.concatenate([index, index[:4]], axis=0)
        edges = []
        for c in range(3):
            halves = []
            for h in range(nodes // 128):
                where = index[:, h * 128:(h + 1) * 128]
                low = lax.rem(where, 128)
                got = None
                for s in range(nodes // 128):
                    pool = jnp.broadcast_to(x[c:c + 1, s * 128:(s + 1) * 128], (16, 128))
                    one = jnp.concatenate([jnp.take_along_axis(pool[k:k + 8], low[k:k + 8], axis=1) for k in (0, 8)], axis=0)
                    got = one if got is None else jnp.where(where >= s * 128, one, got)
                halves.append(got)
            edges.append(jnp.concatenate(halves, axis=1)[:12] - x[c:c + 1])
        square = edges[0][:6] ** 2 + edges[1][:6] ** 2 + edges[2][:6] ** 2
        stretch = square / (length * length)
        tension = (stretch - 1.0) / (stretch + 1.0) / length
        out = []
        for c in range(3):
            surface = modulus[0:1] * jnp.sum(tension * edges[c][:6], axis=0, keepdims=True)
            near = jnp.sum(edges[c][:6], axis=0, keepdims=True) * (2.0 / 9.0)
            far = jnp.sum(edges[c][6:], axis=0, keepdims=True) * (1.0 / 18.0)
            out.append(surface + modulus[1:2] * (near - far - bend[c:c + 1]))
        return jnp.concatenate(out, axis=0)

    send_first(0)
    par_own[...] = par_ref[me]

    @pl.loop(0, STEPS)
    def _(e):
        u = velocity(e)
        x = blk[e][0:3] + TIME_STEP * u

        @pl.when(e == 0)
        def _():
            take_params()

        blk[e + 1] = pack(x, membrane(x))
        send_first(e + 1)

    x_out[...] = blk[STEPS][0:3]
    v_out[...] = velocity(STEPS)
    for e in range(STEPS + 1):
        w = buf.at[e, pl.ds(1, half), pl.ds(0, 6)]
        pltpu.make_async_remote_copy(w, w, send_sem.at[e], recv_sem.at[e, 0], device_id=coords(1), device_id_type=MESH).wait_send()
        w = ret.at[e, pl.ds(0, half - 1)]
        pltpu.make_async_remote_copy(w, w, ret_send.at[e], ret_recv.at[e], device_id=coords(1), device_id_type=MESH).wait_send()
    w = par_buf.at[pl.ds(0, devices - 1)]
    pltpu.make_async_remote_copy(w, w, par_send, par_recv, device_id=coords(1), device_id_type=MESH).wait_send()


def solution(mesh):
    n_tgt, n_src = mesh.shape["tgt"], mesh.shape["src"]
    devices = n_tgt * n_src

    def body(positions, forces, neighbours, patch_owner, rest_length, moduli, rest_bend):
        nodes = positions.shape[1]
        capacity = rest_length.shape[1] // devices
        fields = jnp.concatenate([rest_length, moduli, rest_bend, jnp.zeros_like(moduli[:1])], axis=0)
        table = fields.reshape(FIELDS, devices, capacity).transpose(1, 2, 0).reshape(devices, 1, capacity * FIELDS)
        table = jnp.pad(table, ((0, 0), (0, 0), (0, 128 - capacity * FIELDS)))
        vmem = pl.BlockSpec(memory_space=pltpu.VMEM)
        return pl.pallas_call(
            functools.partial(kernel, n_src, devices, nodes, capacity, 1.0 / math.sqrt(nodes * devices)),
            name="stokes",
            out_shape=(jax.ShapeDtypeStruct((3, nodes), F32), jax.ShapeDtypeStruct((3, nodes), F32)),
            in_specs=[vmem] * 5,
            out_specs=(vmem, vmem),
            scratch_shapes=[
                pltpu.VMEM((STEPS + 1, devices // 2 + 1, 8, nodes), F32),
                pltpu.VMEM((STEPS + 1, 8, nodes), F32),
                pltpu.VMEM((STEPS + 1, devices // 2, 3, nodes), F32),
                pltpu.VMEM((STEPS + 1, devices // 2, 3, nodes), F32),
                pltpu.VMEM((devices, 1, 128), F32),
                pltpu.VMEM((1, 128), F32),
                pltpu.VMEM((16, nodes), F32),
                pltpu.VMEM((3, nodes, 128), F32),
                pltpu.VMEM((2 * nodes, 48), BF16),
                pltpu.VMEM((2, 2 * nodes, nodes), F32),
                pltpu.VMEM((3, nodes, 128), F32),
                pltpu.VMEM((16, nodes), F32),
                pltpu.SemaphoreType.DMA((STEPS + 1,)),
                pltpu.SemaphoreType.DMA((STEPS + 1, devices // 4)),
                pltpu.SemaphoreType.DMA((STEPS + 1,)),
                pltpu.SemaphoreType.DMA((STEPS + 1,)),
                pltpu.SemaphoreType.DMA,
                pltpu.SemaphoreType.DMA,
            ],
            compiler_params=pltpu.CompilerParams(collective_id=0, has_side_effects=True, vmem_limit_bytes=48 * 1024 * 1024),
        )(positions, forces, neighbours, patch_owner.reshape(1, nodes), table)

    cut = P(None, ("tgt", "src"))
    return jax.shard_map(
        body,
        mesh=mesh,
        in_specs=(cut, cut, cut, P(("tgt", "src"), None), cut, cut, cut),
        out_specs=(cut, cut),
        check_vma=False,
    )
```

```python
import functools
import math

import jax
import jax.numpy as jnp
from jax import lax
from jax.experimental import pallas as pl
from jax.experimental.pallas import tpu as pltpu
from jax.sharding import PartitionSpec as P

F32, BF16 = jnp.float32, jnp.bfloat16
MESH = pl.DeviceIdType.MESH
STEPS = 3
UNITS = 20.0
TIME_STEP = 0.5
ROWS = 16
AHEAD = 16
FIELDS = 12


def split3(v):
    high = v.astype(BF16).astype(F32)
    rest = v - high
    middle = rest.astype(BF16).astype(F32)
    return [high.astype(BF16), middle.astype(BF16), (rest - middle).astype(BF16)]


def dot(a, b, dims):
    return lax.dot_general(a, b, (dims, ((), ())), preferred_element_type=F32)


def kernel(n_src, devices, nodes, capacity, scale, pos_ref, frc_ref, nbr_ref, own_ref, par_ref, x_out, v_out,
           buf, blk, ret, out, par_buf, par_own, prm, place, xb, lhs, mine, theirs, prod, acc, near, send_sem, recv_sem, ret_send, ret_recv, par_send, par_recv):
    me = lax.axis_index("tgt") * n_src + lax.axis_index("src")
    half = devices // 2

    shift = n_src.bit_length() - 1

    def coords(k):
        t = (me + k) & (devices - 1)
        return (t >> shift, t & (n_src - 1))

    barrier = pltpu.get_barrier_semaphore()

    def greet(k):
        pl.semaphore_signal(barrier, inc=1, device_id=coords(k), device_id_type=MESH)

    @pl.loop(0, devices // 8 - 1)
    def _(k):
        for i in range(1, 9):
            greet(k * 8 + i)

    for i in range(devices - 7, devices):
        greet(i)

    def pack(x, f):
        return jnp.concatenate([x, f, jnp.sum(x * f, axis=0, keepdims=True), jnp.ones((1, nodes), F32)], axis=0)

    place[...] = pos_ref[...]
    blk[0] = pack(pos_ref[...] * UNITS, frc_ref[...])
    pl.semaphore_wait(barrier, devices - 1)

    def partner(s):
        i, j = (s - 1) & 7, (s - 1) >> 3
        turn = (i >> 1) + (i & 1) * (7 - 2 * (i >> 1))
        last = half // 8 - 1
        return jnp.where(j == last, 8 * (i + 1), 8 * turn + j + 1)

    def send_block(e, s):
        pltpu.make_async_remote_copy(
            src_ref=blk.at[e, pl.ds(0, 6)], dst_ref=buf.at[e, s, pl.ds(0, 6)],
            send_sem=send_sem.at[e], recv_sem=recv_sem.at[e, (s - 1) >> 1],
            device_id=coords(partner(s)), device_id_type=MESH,
        ).start()

    def send_first(e):
        for s in range(1, AHEAD + 1):
            send_block(e, jnp.int32(s))

    def wait_pair(e, m):
        w = buf.at[e, pl.ds(2 * m + 1, 2), pl.ds(0, 6)]
        pltpu.make_async_remote_copy(w, w, send_sem.at[e], recv_sem.at[e, m], device_id=coords(1), device_id_type=MESH).wait_recv()

    def send_params(first, count):
        @pl.loop(first, first + count)
        def _(k):
            t = (me + k) & (devices - 1)

            @pl.when(k < devices)
            def _():
                pltpu.make_async_remote_copy(
                    src_ref=par_ref.at[t], dst_ref=par_buf.at[me], send_sem=par_send, recv_sem=par_recv,
                    device_id=coords(k), device_id_type=MESH,
                ).start()

    def velocity(e):
        own = blk[e]
        buf[e, 0] = own
        own_parts = split3(own)
        parts = jnp.concatenate([p.astype(F32) for p in own_parts], axis=0).astype(BF16)
        row = lax.broadcasted_iota(jnp.int32, (24, 128), 0)
        for c in range(3):
            pick = ((row % 8) == c).astype(F32).astype(BF16)
            xb[c] = dot(parts, pick, ((0,), (0,)))
        none = jnp.zeros((3, nodes), F32)
        one = jnp.ones((1, nodes), F32)
        fields = (jnp.concatenate([none, own[0:3], -one, one * 0.0], axis=0),
                  jnp.concatenate([-own[3:6], none, one * 0.0, own[6:7]], axis=0))
        for i, field in enumerate(fields):
            h, m, l = [p.astype(F32) for p in split3(field)]
            lhs[i * nodes:(i + 1) * nodes, :] = jnp.concatenate([h, h, m, m, h, l], axis=0).T.astype(BF16)
        acc[...] = jnp.zeros_like(acc)
        near[...] = jnp.zeros_like(near)

        def expand(g):
            return [p.astype(F32) for p in split3(pack(g[0:3], g[3:6]))]

        def products(g, p):
            h, m, l = expand(g)
            prod[p] = dot(lhs[...], jnp.concatenate([h, m, h, m, l, h], axis=0).astype(BF16), ((1,), (0,)))
            theirs[p] = jnp.concatenate([h, m], axis=0).astype(BF16)

        h, m, _ = [p.astype(F32) for p in own_parts]
        mine[...] = jnp.concatenate([h, m], axis=0).astype(BF16)

        def pair(g, p, both):
            high, low = [], []
            back = [[None] * 3 for _ in range(nodes // 128)]
            for r in range(0, nodes, ROWS):
                rows = slice(r, r + ROWS)
                total = [acc[c, rows, :] for c in range(3)]
                highs, lows = [], []
                for h in range(nodes // 128):
                    cols = slice(h * 128, (h + 1) * 128)
                    d = [xb[c, rows, :] - g[c:c + 1, cols] for c in range(3)]
                    q = d[0] * d[0] + (d[1] * d[1] + (d[2] * d[2] + 1.0))
                    w = lax.rsqrt(q)
                    w3 = w * w * w
                    direct = w + w3
                    t = prod[p, rows, cols] * w3
                    for c in range(3):
                        total[c] = total[c] + t * d[c]
                    if both:
                        t = prod[p, nodes + r:nodes + r + ROWS, cols] * w3
                        for c in range(3):
                            v = t * d[c]
                            for k in range(0, ROWS, 8):
                                back[h][c] = v[k:k + 8] if back[h][c] is None else back[h][c] + v[k:k + 8]
                    top = direct.astype(BF16)
                    highs.append(top)
                    lows.append((direct - top.astype(F32)).astype(BF16))
                for c in range(3):
                    acc[c, rows, :] = total[c]
                high.append(jnp.concatenate(highs, axis=1))
                low.append(jnp.concatenate(lows, axis=1))
            high, low = jnp.concatenate(high, axis=0), jnp.concatenate(low, axis=0)
            near[...] += dot(theirs[p], high, ((1,), (1,))) + dot(theirs[p], low, ((1,), (1,)))
            if not both:
                return None
            rev = dot(mine[...], high, ((1,), (0,))) + dot(mine[...], low, ((1,), (0,)))
            along = [jnp.concatenate([jnp.sum(b[c], axis=0, keepdims=True) for b in back], axis=1) for c in range(3)]
            return jnp.concatenate(along, axis=0) + rev[3:6] + rev[11:14]

        def give_back(s):
            k = partner(s)

            @pl.when((s > 0) & (s < half))
            def _():
                pltpu.make_async_remote_copy(
                    src_ref=out.at[e, s], dst_ref=ret.at[e, k - 1],
                    send_sem=ret_send.at[e], recv_sem=ret_recv.at[e],
                    device_id=coords(devices - k), device_id_type=MESH,
                ).start()

        products(own, 0)

        @pl.loop(0, half // 2)
        def _(m):
            s = m * 2

            @pl.when(m < (half - AHEAD) // 2)
            def _():
                send_block(e, AHEAD + 1 + s)
                send_block(e, AHEAD + 2 + s)

            if e is not STEPS:
                @pl.when(e == 0)
                def _():
                    send_params(1 + m * 4, 4)

            @pl.when(m > 0)
            def _():
                give_back(s - 2)
                give_back(s - 1)

            wait_pair(e, m)
            products(buf[e, s + 1, 0:6], 1)
            out[e, s] = pair(buf[e, s, 0:6], 0, True)
            products(buf[e, s + 2, 0:6], 0)
            out[e, s + 1] = pair(buf[e, s + 1, 0:6], 1, True)

        give_back(jnp.int32(half - 2))
        give_back(jnp.int32(half - 1))
        pair(buf[e, half, 0:6], 0, False)

        ones = jnp.ones((8, 128), BF16)
        total = []
        for c in range(3):
            total.append(sum(dot(ones, p, ((1,), (1,))) for p in split3(acc[c]))[0:1])
        total = jnp.concatenate(total, axis=0) + near[3:6] + near[11:14]
        w = ret.at[e, pl.ds(0, half - 1)]
        pltpu.make_async_remote_copy(w, w, ret_send.at[e], ret_recv.at[e], device_id=coords(1), device_id_type=MESH).wait_recv()
        total = total + jnp.sum(ret[e, 0:half - 1], axis=0)
        return total * (scale * UNITS)

    def take_params():
        w = par_buf.at[pl.ds(0, devices - 1)]
        pltpu.make_async_remote_copy(w, w, par_send, par_recv, device_id=coords(1), device_id_type=MESH).wait_recv()
        par_buf[me] = par_own[...]
        table = par_buf[...].reshape(devices, 128)
        owner = own_ref[...]
        hot = (lax.broadcasted_iota(jnp.int32, (devices, nodes), 0) == owner).astype(F32)
        hot16 = hot.astype(BF16)
        earlier = (lax.broadcasted_iota(jnp.int32, (nodes, nodes), 0) < lax.broadcasted_iota(jnp.int32, (nodes, nodes), 1))
        before = dot(hot16, earlier.astype(F32).astype(BF16), ((1,), (0,)))
        rank = jnp.sum(before * hot, axis=0, keepdims=True)
        rows = sum(dot(p, hot16, ((0,), (0,))) for p in split3(table))
        place = lax.broadcasted_iota(jnp.int32, (128, nodes), 0)
        base = rank.astype(jnp.int32) * FIELDS
        rows = jnp.where((place >= base) & (place < base + FIELDS), rows, 0.0)
        fold = ((lax.broadcasted_iota(jnp.int32, (16, 128), 1) % FIELDS) == lax.broadcasted_iota(jnp.int32, (16, 128), 0))
        fold = fold.astype(F32).astype(BF16)
        prm[...] = sum(dot(fold, p, ((1,), (0,))) for p in split3(rows))

    def membrane(x):
        length, modulus, bend = prm[0:6], prm[6:8], prm[8:11]
        index = nbr_ref[...]
        index = jnp.concatenate([index, index[:4]], axis=0)
        edges = []
        for c in range(3):
            halves = []
            for h in range(nodes // 128):
                where = index[:, h * 128:(h + 1) * 128]
                low = lax.rem(where, 128)
                got = None
                for s in range(nodes // 128):
                    pool = jnp.broadcast_to(x[c:c + 1, s * 128:(s + 1) * 128], (16, 128))
                    one = jnp.concatenate([jnp.take_along_axis(pool[k:k + 8], low[k:k + 8], axis=1) for k in (0, 8)], axis=0)
                    got = one if got is None else jnp.where(where >= s * 128, one, got)
                halves.append(got)
            edges.append(jnp.concatenate(halves, axis=1)[:12] - x[c:c + 1])
        square = edges[0][:6] ** 2 + edges[1][:6] ** 2 + edges[2][:6] ** 2
        stretch = square / (length * length)
        tension = (stretch - 1.0) / (stretch + 1.0) / length
        out = []
        for c in range(3):
            surface = modulus[0:1] * jnp.sum(tension * edges[c][:6], axis=0, keepdims=True)
            near = jnp.sum(edges[c][:6], axis=0, keepdims=True) * (2.0 / 9.0)
            far = jnp.sum(edges[c][6:], axis=0, keepdims=True) * (1.0 / 18.0)
            out.append(surface + modulus[1:2] * (near - far - bend[c:c + 1]))
        return jnp.concatenate(out, axis=0)

    send_first(0)
    par_own[...] = par_ref[me]

    @pl.loop(0, STEPS)
    def _(e):
        u = velocity(e)
        x = place[...] + TIME_STEP * u
        place[...] = x

        @pl.when(e == 0)
        def _():
            take_params()

        blk[e + 1] = pack(x * UNITS, membrane(x))
        send_first(e + 1)

    x_out[...] = place[...]
    v_out[...] = velocity(STEPS)
    for e in range(STEPS + 1):
        w = buf.at[e, pl.ds(1, half), pl.ds(0, 6)]
        pltpu.make_async_remote_copy(w, w, send_sem.at[e], recv_sem.at[e, 0], device_id=coords(1), device_id_type=MESH).wait_send()
        w = ret.at[e, pl.ds(0, half - 1)]
        pltpu.make_async_remote_copy(w, w, ret_send.at[e], ret_recv.at[e], device_id=coords(1), device_id_type=MESH).wait_send()
    w = par_buf.at[pl.ds(0, devices - 1)]
    pltpu.make_async_remote_copy(w, w, par_send, par_recv, device_id=coords(1), device_id_type=MESH).wait_send()


def solution(mesh):
    n_tgt, n_src = mesh.shape["tgt"], mesh.shape["src"]
    devices = n_tgt * n_src

    def body(positions, forces, neighbours, patch_owner, rest_length, moduli, rest_bend):
        nodes = positions.shape[1]
        capacity = rest_length.shape[1] // devices
        fields = jnp.concatenate([rest_length, moduli, rest_bend, jnp.zeros_like(moduli[:1])], axis=0)
        table = fields.reshape(FIELDS, devices, capacity).transpose(1, 2, 0).reshape(devices, 1, capacity * FIELDS)
        table = jnp.pad(table, ((0, 0), (0, 0), (0, 128 - capacity * FIELDS)))
        vmem = pl.BlockSpec(memory_space=pltpu.VMEM)
        return pl.pallas_call(
            functools.partial(kernel, n_src, devices, nodes, capacity, 1.0 / math.sqrt(nodes * devices)),
            name="stokes",
            out_shape=(jax.ShapeDtypeStruct((3, nodes), F32), jax.ShapeDtypeStruct((3, nodes), F32)),
            in_specs=[vmem] * 5,
            out_specs=(vmem, vmem),
            scratch_shapes=[
                pltpu.VMEM((STEPS + 1, devices // 2 + 1, 8, nodes), F32),
                pltpu.VMEM((STEPS + 1, 8, nodes), F32),
                pltpu.VMEM((STEPS + 1, devices // 2, 3, nodes), F32),
                pltpu.VMEM((STEPS + 1, devices // 2, 3, nodes), F32),
                pltpu.VMEM((devices, 1, 128), F32),
                pltpu.VMEM((1, 128), F32),
                pltpu.VMEM((16, nodes), F32),
                pltpu.VMEM((3, nodes), F32),
                pltpu.VMEM((3, nodes, 128), F32),
                pltpu.VMEM((2 * nodes, 48), BF16),
                pltpu.VMEM((16, nodes), BF16),
                pltpu.VMEM((2, 16, nodes), BF16),
                pltpu.VMEM((2, 2 * nodes, nodes), F32),
                pltpu.VMEM((3, nodes, 128), F32),
                pltpu.VMEM((16, nodes), F32),
                pltpu.SemaphoreType.DMA((STEPS + 1,)),
                pltpu.SemaphoreType.DMA((STEPS + 1, devices // 4)),
                pltpu.SemaphoreType.DMA((STEPS + 1,)),
                pltpu.SemaphoreType.DMA((STEPS + 1,)),
                pltpu.SemaphoreType.DMA,
                pltpu.SemaphoreType.DMA,
            ],
            compiler_params=pltpu.CompilerParams(collective_id=0, has_side_effects=True, vmem_limit_bytes=48 * 1024 * 1024),
        )(positions, forces, neighbours, patch_owner.reshape(1, nodes), table)

    cut = P(None, ("tgt", "src"))
    return jax.shard_map(
        body,
        mesh=mesh,
        in_specs=(cut, cut, cut, P(("tgt", "src"), None), cut, cut, cut),
        out_specs=(cut, cut),
        check_vma=False,
    )
```

```python
import functools
import math

import jax
import jax.numpy as jnp
from jax import lax
from jax.experimental import pallas as pl
from jax.experimental.pallas import tpu as pltpu
from jax.sharding import PartitionSpec as P

F32, BF16 = jnp.float32, jnp.bfloat16
MESH = pl.DeviceIdType.MESH
STEPS = 3
UNITS = 20.0
TIME_STEP = 0.5
ROWS = 16
AHEAD = 32
FIELDS = 12


def split3(v):
    high = v.astype(BF16).astype(F32)
    rest = v - high
    middle = rest.astype(BF16).astype(F32)
    return [high.astype(BF16), middle.astype(BF16), (rest - middle).astype(BF16)]


def dot(a, b, dims):
    return lax.dot_general(a, b, (dims, ((), ())), preferred_element_type=F32)


def kernel(n_src, devices, nodes, capacity, scale, pos_ref, frc_ref, nbr_ref, own_ref, par_ref, x_out, v_out,
           buf, blk, ret, out, par_buf, par_own, prm, place, xb, lhs, mine, theirs, prod, acc, near, send_sem, recv_sem, ret_send, ret_recv, par_send, par_recv):
    me = lax.axis_index("tgt") * n_src + lax.axis_index("src")
    half = devices // 2

    shift = n_src.bit_length() - 1

    def coords(k):
        t = (me + k) & (devices - 1)
        return (t >> shift, t & (n_src - 1))

    barrier = pltpu.get_barrier_semaphore()

    def greet(k):
        pl.semaphore_signal(barrier, inc=1, device_id=coords(k), device_id_type=MESH)

    @pl.loop(0, devices // 8 - 1)
    def _(k):
        for i in range(1, 9):
            greet(k * 8 + i)

    for i in range(devices - 7, devices):
        greet(i)

    def pack(x, f):
        return jnp.concatenate([x, f, jnp.sum(x * f, axis=0, keepdims=True), jnp.ones((1, nodes), F32)], axis=0)

    place[...] = pos_ref[...]
    blk[0] = pack(pos_ref[...] * UNITS, frc_ref[...])

    def partner(s):
        u = s - 3
        i = u & 7
        k = 8 * ((i >> 1) + (i & 1) * (7 - 2 * (i >> 1))) + (u >> 3) + 1
        v = s - (half - 5)
        step = 8 * ((v + 1) >> 1)
        k = jnp.where(v >= 0, half // 2 + jnp.where((v & 1) == 1, -step, step), k)
        k = jnp.where(s == half, half, k)
        return jnp.where(s <= 2, jnp.where(s == 1, 8, half - 8), k)

    def send_block(e, s, where):
        pltpu.make_async_remote_copy(
            src_ref=blk.at[e, pl.ds(0, 6)], dst_ref=buf.at[e, s, pl.ds(0, 6)],
            send_sem=send_sem.at[e], recv_sem=recv_sem.at[e, (s - 1) >> 1],
            device_id=where, device_id_type=MESH,
        ).start()

    def send_first(e):
        for s in range(1, AHEAD + 1):
            send_block(e, s, coords(partner(jnp.int32(s))))

    def wait_pair(e, m):
        w = buf.at[e, pl.ds(2 * m + 1, 2), pl.ds(0, 6)]
        pltpu.make_async_remote_copy(w, w, send_sem.at[e], recv_sem.at[e, m], device_id=coords(1), device_id_type=MESH).wait_recv()

    def send_params(first, count):
        @pl.loop(first, first + count)
        def _(k):
            t = (me + k) & (devices - 1)

            @pl.when(k < devices)
            def _():
                pltpu.make_async_remote_copy(
                    src_ref=par_ref.at[t], dst_ref=par_buf.at[me], send_sem=par_send, recv_sem=par_recv,
                    device_id=coords(k), device_id_type=MESH,
                ).start()

    def expand(g):
        return [p.astype(F32) for p in split3(pack(g[0:3], g[3:6]))]

    def products(g, p):
        h, m, l = expand(g)
        prod[p] = dot(lhs[...], jnp.concatenate([h, m, h, m, l, h], axis=0).astype(BF16), ((1,), (0,)))
        theirs[p] = jnp.concatenate([h, m], axis=0).astype(BF16)

    def prepare(e):
        own = blk[e]
        buf[e, 0] = own
        own_parts = split3(own)
        parts = jnp.concatenate([p.astype(F32) for p in own_parts], axis=0).astype(BF16)
        row = lax.broadcasted_iota(jnp.int32, (24, 128), 0)
        for c in range(3):
            pick = ((row % 8) == c).astype(F32).astype(BF16)
            xb[c] = dot(parts, pick, ((0,), (0,)))
        none = jnp.zeros((3, nodes), F32)
        one = jnp.ones((1, nodes), F32)
        fields = (jnp.concatenate([none, own[0:3], -one, one * 0.0], axis=0),
                  jnp.concatenate([-own[3:6], none, one * 0.0, own[6:7]], axis=0))
        for i, field in enumerate(fields):
            h, m, l = [p.astype(F32) for p in split3(field)]
            lhs[i * nodes:(i + 1) * nodes, :] = jnp.concatenate([h, h, m, m, h, l], axis=0).T.astype(BF16)
        acc[...] = jnp.zeros_like(acc)
        near[...] = jnp.zeros_like(near)

        h, m, _ = [p.astype(F32) for p in own_parts]
        mine[...] = jnp.concatenate([h, m], axis=0).astype(BF16)
        products(own, 0)

    def velocity(e):
        def pair(g, p, both):
            high, low = [], []
            back = [[None] * 3 for _ in range(nodes // 128)]
            for r in range(0, nodes, ROWS):
                rows = slice(r, r + ROWS)
                total = [acc[c, rows, :] for c in range(3)]
                highs, lows = [], []
                for h in range(nodes // 128):
                    cols = slice(h * 128, (h + 1) * 128)
                    d = [xb[c, rows, :] - g[c:c + 1, cols] for c in range(3)]
                    q = d[0] * d[0] + (d[1] * d[1] + (d[2] * d[2] + 1.0))
                    w = lax.rsqrt(q)
                    w3 = w * w * w
                    direct = w + w3
                    t = prod[p, rows, cols] * w3
                    for c in range(3):
                        total[c] = total[c] + t * d[c]
                    if both:
                        t = prod[p, nodes + r:nodes + r + ROWS, cols] * w3
                        for c in range(3):
                            v = t * d[c]
                            for k in range(0, ROWS, 8):
                                back[h][c] = v[k:k + 8] if back[h][c] is None else back[h][c] + v[k:k + 8]
                    top = direct.astype(BF16)
                    highs.append(top)
                    lows.append((direct - top.astype(F32)).astype(BF16))
                for c in range(3):
                    acc[c, rows, :] = total[c]
                high.append(jnp.concatenate(highs, axis=1))
                low.append(jnp.concatenate(lows, axis=1))
            high, low = jnp.concatenate(high, axis=0), jnp.concatenate(low, axis=0)
            near[...] += dot(theirs[p], high, ((1,), (1,))) + dot(theirs[p], low, ((1,), (1,)))
            if not both:
                return None
            rev = dot(mine[...], high, ((1,), (0,))) + dot(mine[...], low, ((1,), (0,)))
            along = [jnp.concatenate([jnp.sum(b[c], axis=0, keepdims=True) for b in back], axis=1) for c in range(3)]
            return jnp.concatenate(along, axis=0) + rev[3:6] + rev[11:14]

        def give_back(s, k, where):
            pltpu.make_async_remote_copy(
                src_ref=out.at[e, s], dst_ref=ret.at[e, k - 1],
                send_sem=ret_send.at[e], recv_sem=ret_recv.at[e],
                device_id=where, device_id_type=MESH,
            ).start()

        def targets(m):
            s = m * 2
            k1, k2 = partner(s - 2), partner(s - 1)
            return (coords(partner(AHEAD + 1 + s)) + coords(partner(AHEAD + 2 + s))
                    + (k1, k2) + coords(devices - k1) + coords(devices - k2))

        def step(m, at):
            s = m * 2

            @pl.when(m < (half - AHEAD) // 2)
            def _():
                send_block(e, AHEAD + 1 + s, at[0:2])
                send_block(e, AHEAD + 2 + s, at[2:4])

            if e is not STEPS:
                @pl.when(e == 0)
                def _():
                    send_params(1 + m * 4, 4)

            @pl.when(m > 1)
            def _():
                give_back(s - 2, at[4], at[6:8])

            @pl.when(m > 0)
            def _():
                give_back(s - 1, at[5], at[8:10])

            wait_pair(e, m)
            products(buf[e, s + 1, 0:6], 1)
            out[e, s] = pair(buf[e, s, 0:6], 0, True)
            products(buf[e, s + 2, 0:6], 0)
            out[e, s + 1] = pair(buf[e, s + 1, 0:6], 1, True)
            return targets(m + 1)

        lax.fori_loop(0, half // 2, step, targets(jnp.int32(0)))
        for s in (half - 2, half - 1):
            k = partner(jnp.int32(s))
            give_back(s, k, coords(devices - k))
        pair(buf[e, half, 0:6], 0, False)

        ones = jnp.ones((8, 128), BF16)
        total = []
        for c in range(3):
            total.append(sum(dot(ones, p, ((1,), (1,))) for p in split3(acc[c]))[0:1])
        total = jnp.concatenate(total, axis=0) + near[3:6] + near[11:14]
        w = ret.at[e, pl.ds(0, half - 1)]
        pltpu.make_async_remote_copy(w, w, ret_send.at[e], ret_recv.at[e], device_id=coords(1), device_id_type=MESH).wait_recv()
        total = total + jnp.sum(ret[e, 0:half - 1], axis=0)
        return total * (scale * UNITS)

    def take_params():
        w = par_buf.at[pl.ds(0, devices - 1)]
        pltpu.make_async_remote_copy(w, w, par_send, par_recv, device_id=coords(1), device_id_type=MESH).wait_recv()
        par_buf[me] = par_own[...]
        table = par_buf[...].reshape(devices, 128)
        owner = own_ref[...]
        hot = (lax.broadcasted_iota(jnp.int32, (devices, nodes), 0) == owner).astype(F32)
        hot16 = hot.astype(BF16)
        earlier = (lax.broadcasted_iota(jnp.int32, (nodes, nodes), 0) < lax.broadcasted_iota(jnp.int32, (nodes, nodes), 1))
        before = dot(hot16, earlier.astype(F32).astype(BF16), ((1,), (0,)))
        rank = jnp.sum(before * hot, axis=0, keepdims=True)
        rows = sum(dot(p, hot16, ((0,), (0,))) for p in split3(table))
        place = lax.broadcasted_iota(jnp.int32, (128, nodes), 0)
        base = rank.astype(jnp.int32) * FIELDS
        rows = jnp.where((place >= base) & (place < base + FIELDS), rows, 0.0)
        fold = ((lax.broadcasted_iota(jnp.int32, (16, 128), 1) % FIELDS) == lax.broadcasted_iota(jnp.int32, (16, 128), 0))
        fold = fold.astype(F32).astype(BF16)
        prm[...] = sum(dot(fold, p, ((1,), (0,))) for p in split3(rows))

    def membrane(x):
        length, modulus, bend = prm[0:6], prm[6:8], prm[8:11]
        index = nbr_ref[...]
        index = jnp.concatenate([index, index[:4]], axis=0)
        edges = []
        for c in range(3):
            halves = []
            for h in range(nodes // 128):
                where = index[:, h * 128:(h + 1) * 128]
                low = lax.rem(where, 128)
                got = None
                for s in range(nodes // 128):
                    pool = jnp.broadcast_to(x[c:c + 1, s * 128:(s + 1) * 128], (16, 128))
                    one = jnp.concatenate([jnp.take_along_axis(pool[k:k + 8], low[k:k + 8], axis=1) for k in (0, 8)], axis=0)
                    got = one if got is None else jnp.where(where >= s * 128, one, got)
                halves.append(got)
            edges.append(jnp.concatenate(halves, axis=1)[:12] - x[c:c + 1])
        square = edges[0][:6] ** 2 + edges[1][:6] ** 2 + edges[2][:6] ** 2
        stretch = square / (length * length)
        tension = (stretch - 1.0) / (stretch + 1.0) / length
        out = []
        for c in range(3):
            surface = modulus[0:1] * jnp.sum(tension * edges[c][:6], axis=0, keepdims=True)
            near = jnp.sum(edges[c][:6], axis=0, keepdims=True) * (2.0 / 9.0)
            far = jnp.sum(edges[c][6:], axis=0, keepdims=True) * (1.0 / 18.0)
            out.append(surface + modulus[1:2] * (near - far - bend[c:c + 1]))
        return jnp.concatenate(out, axis=0)

    prepare(0)
    pl.semaphore_wait(barrier, devices - 1)
    send_first(0)
    par_own[...] = par_ref[me]

    @pl.loop(0, STEPS)
    def _(e):
        u = velocity(e)
        x = place[...] + TIME_STEP * u
        place[...] = x

        @pl.when(e == 0)
        def _():
            take_params()

        blk[e + 1] = pack(x * UNITS, membrane(x))
        send_first(e + 1)
        prepare(e + 1)

    x_out[...] = place[...]
    v_out[...] = velocity(STEPS)
    for e in range(STEPS + 1):
        w = buf.at[e, pl.ds(1, half), pl.ds(0, 6)]
        pltpu.make_async_remote_copy(w, w, send_sem.at[e], recv_sem.at[e, 0], device_id=coords(1), device_id_type=MESH).wait_send()
        w = ret.at[e, pl.ds(0, half - 1)]
        pltpu.make_async_remote_copy(w, w, ret_send.at[e], ret_recv.at[e], device_id=coords(1), device_id_type=MESH).wait_send()
    w = par_buf.at[pl.ds(0, devices - 1)]
    pltpu.make_async_remote_copy(w, w, par_send, par_recv, device_id=coords(1), device_id_type=MESH).wait_send()


def solution(mesh):
    n_tgt, n_src = mesh.shape["tgt"], mesh.shape["src"]
    devices = n_tgt * n_src

    def body(positions, forces, neighbours, patch_owner, rest_length, moduli, rest_bend):
        nodes = positions.shape[1]
        capacity = rest_length.shape[1] // devices
        fields = jnp.concatenate([rest_length, moduli, rest_bend, jnp.zeros_like(moduli[:1])], axis=0)
        table = fields.reshape(FIELDS, devices, capacity).transpose(1, 2, 0).reshape(devices, 1, capacity * FIELDS)
        table = jnp.pad(table, ((0, 0), (0, 0), (0, 128 - capacity * FIELDS)))
        vmem = pl.BlockSpec(memory_space=pltpu.VMEM)
        return pl.pallas_call(
            functools.partial(kernel, n_src, devices, nodes, capacity, 1.0 / math.sqrt(nodes * devices)),
            name="stokes",
            out_shape=(jax.ShapeDtypeStruct((3, nodes), F32), jax.ShapeDtypeStruct((3, nodes), F32)),
            in_specs=[vmem] * 5,
            out_specs=(vmem, vmem),
            scratch_shapes=[
                pltpu.VMEM((STEPS + 1, devices // 2 + 1, 8, nodes), F32),
                pltpu.VMEM((STEPS + 1, 8, nodes), F32),
                pltpu.VMEM((STEPS + 1, devices // 2, 3, nodes), F32),
                pltpu.VMEM((STEPS + 1, devices // 2, 3, nodes), F32),
                pltpu.VMEM((devices, 1, 128), F32),
                pltpu.VMEM((1, 128), F32),
                pltpu.VMEM((16, nodes), F32),
                pltpu.VMEM((3, nodes), F32),
                pltpu.VMEM((3, nodes, 128), F32),
                pltpu.VMEM((2 * nodes, 48), BF16),
                pltpu.VMEM((16, nodes), BF16),
                pltpu.VMEM((2, 16, nodes), BF16),
                pltpu.VMEM((2, 2 * nodes, nodes), F32),
                pltpu.VMEM((3, nodes, 128), F32),
                pltpu.VMEM((16, nodes), F32),
                pltpu.SemaphoreType.DMA((STEPS + 1,)),
                pltpu.SemaphoreType.DMA((STEPS + 1, devices // 4)),
                pltpu.SemaphoreType.DMA((STEPS + 1,)),
                pltpu.SemaphoreType.DMA((STEPS + 1,)),
                pltpu.SemaphoreType.DMA,
                pltpu.SemaphoreType.DMA,
            ],
            compiler_params=pltpu.CompilerParams(collective_id=0, has_side_effects=True, vmem_limit_bytes=48 * 1024 * 1024),
        )(positions, forces, neighbours, patch_owner.reshape(1, nodes), table)

    cut = P(None, ("tgt", "src"))
    return jax.shard_map(
        body,
        mesh=mesh,
        in_specs=(cut, cut, cut, P(("tgt", "src"), None), cut, cut, cut),
        out_specs=(cut, cut),
        check_vma=False,
    )
```

```python
import functools
import math

import jax
import jax.numpy as jnp
from jax import lax
from jax.experimental import pallas as pl
from jax.experimental.pallas import tpu as pltpu
from jax.sharding import PartitionSpec as P

F32, BF16 = jnp.float32, jnp.bfloat16
MESH = pl.DeviceIdType.MESH
STEPS = 3
UNITS = 20.0
TIME_STEP = 0.5
ROWS = 16
AHEAD = 24
FIELDS = 12


def split3(v):
    high = v.astype(BF16).astype(F32)
    rest = v - high
    middle = rest.astype(BF16).astype(F32)
    return [high.astype(BF16), middle.astype(BF16), (rest - middle).astype(BF16)]


def dot(a, b, dims):
    return lax.dot_general(a, b, (dims, ((), ())), preferred_element_type=F32)


def kernel(n_src, devices, nodes, capacity, scale, pos_ref, frc_ref, nbr_ref, own_ref, par_ref, x_out, v_out,
           buf, blk, ret, out, par_buf, par_own, prm, place, xb, lhs, mine, theirs, prod, acc, near, send_sem, recv_sem, ret_send, ret_recv, par_send, par_recv):
    me = lax.axis_index("tgt") * n_src + lax.axis_index("src")
    half = devices // 2

    shift = n_src.bit_length() - 1

    def coords(k):
        t = (me + k) & (devices - 1)
        return (t >> shift, t & (n_src - 1))

    barrier = pltpu.get_barrier_semaphore()

    def greet(k):
        pl.semaphore_signal(barrier, inc=1, device_id=coords(k), device_id_type=MESH)

    @pl.loop(0, devices // 8 - 1)
    def _(k):
        for i in range(1, 9):
            greet(k * 8 + i)

    for i in range(devices - 7, devices):
        greet(i)

    def pack(x, f):
        return jnp.concatenate([x, f, jnp.sum(x * f, axis=0, keepdims=True), jnp.ones((1, nodes), F32)], axis=0)

    place[...] = pos_ref[...]
    blk[0] = pack(pos_ref[...] * UNITS, frc_ref[...])

    def partner(s):
        u = s - 3
        i = u & 7
        k = 8 * ((i >> 1) + (i & 1) * (7 - 2 * (i >> 1))) + (u >> 3) + 1
        v = s - (half - 5)
        step = 8 * ((v + 1) >> 1)
        k = jnp.where(v >= 0, half // 2 + jnp.where((v & 1) == 1, -step, step), k)
        k = jnp.where(s == half, half, k)
        return jnp.where(s <= 2, jnp.where(s == 1, 8, half - 8), k)

    def send_block(e, s, where):
        pltpu.make_async_remote_copy(
            src_ref=blk.at[e, pl.ds(0, 6)], dst_ref=buf.at[e, s, pl.ds(0, 6)],
            send_sem=send_sem.at[e], recv_sem=recv_sem.at[e, (s - 1) >> 1],
            device_id=where, device_id_type=MESH,
        ).start()

    def send_first(e):
        for s in range(1, AHEAD + 1):
            send_block(e, s, coords(partner(jnp.int32(s))))

    def wait_pair(e, m):
        w = buf.at[e, pl.ds(2 * m + 1, 2), pl.ds(0, 6)]
        pltpu.make_async_remote_copy(w, w, send_sem.at[e], recv_sem.at[e, m], device_id=coords(1), device_id_type=MESH).wait_recv()

    def send_params(first, count):
        @pl.loop(first, first + count)
        def _(k):
            t = (me + k) & (devices - 1)

            @pl.when(k < devices)
            def _():
                pltpu.make_async_remote_copy(
                    src_ref=par_ref.at[t], dst_ref=par_buf.at[me], send_sem=par_send, recv_sem=par_recv,
                    device_id=coords(k), device_id_type=MESH,
                ).start()

    def expand(g):
        return [p.astype(F32) for p in split3(pack(g[0:3], g[3:6]))]

    def products(g, p):
        h, m, l = expand(g)
        prod[p] = dot(lhs[...], jnp.concatenate([h, m, h, m, l, h], axis=0).astype(BF16), ((1,), (0,)))
        theirs[p] = jnp.concatenate([h, m], axis=0).astype(BF16)

    def prepare(e):
        own = blk[e]
        buf[e, 0] = own
        own_parts = split3(own)
        parts = jnp.concatenate([p.astype(F32) for p in own_parts], axis=0).astype(BF16)
        row = lax.broadcasted_iota(jnp.int32, (24, 128), 0)
        for c in range(3):
            pick = ((row % 8) == c).astype(F32).astype(BF16)
            xb[c] = dot(parts, pick, ((0,), (0,)))
        none = jnp.zeros((3, nodes), F32)
        one = jnp.ones((1, nodes), F32)
        fields = (jnp.concatenate([none, own[0:3], -one, one * 0.0], axis=0),
                  jnp.concatenate([-own[3:6], none, one * 0.0, own[6:7]], axis=0))
        for i, field in enumerate(fields):
            h, m, l = [p.astype(F32) for p in split3(field)]
            lhs[i * nodes:(i + 1) * nodes, :] = jnp.concatenate([h, h, m, m, h, l], axis=0).T.astype(BF16)
        acc[...] = jnp.zeros_like(acc)
        near[...] = jnp.zeros_like(near)

        h, m, _ = [p.astype(F32) for p in own_parts]
        mine[...] = jnp.concatenate([h, m], axis=0).astype(BF16)
        products(own, 0)

    def velocity(e):
        def pair(g, p, both):
            high, low = [], []
            back = [[None] * 3 for _ in range(nodes // 128)]
            for r in range(0, nodes, ROWS):
                rows = slice(r, r + ROWS)
                total = [acc[c, rows, :] for c in range(3)]
                highs, lows = [], []
                for h in range(nodes // 128):
                    cols = slice(h * 128, (h + 1) * 128)
                    d = [xb[c, rows, :] - g[c:c + 1, cols] for c in range(3)]
                    q = d[0] * d[0] + (d[1] * d[1] + (d[2] * d[2] + 1.0))
                    w = lax.rsqrt(q)
                    w3 = w * w * w
                    direct = w + w3
                    t = prod[p, rows, cols] * w3
                    for c in range(3):
                        total[c] = total[c] + t * d[c]
                    if both:
                        t = prod[p, nodes + r:nodes + r + ROWS, cols] * w3
                        for c in range(3):
                            v = t * d[c]
                            for k in range(0, ROWS, 8):
                                back[h][c] = v[k:k + 8] if back[h][c] is None else back[h][c] + v[k:k + 8]
                    top = direct.astype(BF16)
                    highs.append(top)
                    lows.append((direct - top.astype(F32)).astype(BF16))
                for c in range(3):
                    acc[c, rows, :] = total[c]
                high.append(jnp.concatenate(highs, axis=1))
                low.append(jnp.concatenate(lows, axis=1))
            high, low = jnp.concatenate(high, axis=0), jnp.concatenate(low, axis=0)
            near[...] += dot(theirs[p], high, ((1,), (1,))) + dot(theirs[p], low, ((1,), (1,)))
            if not both:
                return None
            rev = dot(mine[...], high, ((1,), (0,))) + dot(mine[...], low, ((1,), (0,)))
            along = [jnp.concatenate([jnp.sum(b[c], axis=0, keepdims=True) for b in back], axis=1) for c in range(3)]
            return jnp.concatenate(along, axis=0) + rev[3:6] + rev[11:14]

        def give_back(s, k, where):
            pltpu.make_async_remote_copy(
                src_ref=out.at[e, s], dst_ref=ret.at[e, k - 1],
                send_sem=ret_send.at[e], recv_sem=ret_recv.at[e],
                device_id=where, device_id_type=MESH,
            ).start()

        def targets(m):
            s = m * 2
            k1, k2 = partner(s - 2), partner(s - 1)
            return (coords(partner(AHEAD + 1 + s)) + coords(partner(AHEAD + 2 + s))
                    + (k1, k2) + coords(devices - k1) + coords(devices - k2))

        def step(m, at):
            s = m * 2

            @pl.when(m < (half - AHEAD) // 2)
            def _():
                send_block(e, AHEAD + 1 + s, at[0:2])
                send_block(e, AHEAD + 2 + s, at[2:4])

            if e is not STEPS:
                @pl.when(e == 0)
                def _():
                    send_params(1 + m * 4, 4)

            @pl.when(m > 1)
            def _():
                give_back(s - 2, at[4], at[6:8])

            @pl.when(m > 0)
            def _():
                give_back(s - 1, at[5], at[8:10])

            wait_pair(e, m)
            products(buf[e, s + 1, 0:6], 1)
            out[e, s] = pair(buf[e, s, 0:6], 0, True)
            products(buf[e, s + 2, 0:6], 0)
            out[e, s + 1] = pair(buf[e, s + 1, 0:6], 1, True)
            return targets(m + 1)

        lax.fori_loop(0, half // 2, step, targets(jnp.int32(0)))
        for s in (half - 2, half - 1):
            k = partner(jnp.int32(s))
            give_back(s, k, coords(devices - k))
        pair(buf[e, half, 0:6], 0, False)

        ones = jnp.ones((8, 128), BF16)
        total = []
        for c in range(3):
            total.append(sum(dot(ones, p, ((1,), (1,))) for p in split3(acc[c]))[0:1])
        total = jnp.concatenate(total, axis=0) + near[3:6] + near[11:14]
        w = ret.at[e, pl.ds(0, half - 1)]
        pltpu.make_async_remote_copy(w, w, ret_send.at[e], ret_recv.at[e], device_id=coords(1), device_id_type=MESH).wait_recv()
        total = total + jnp.sum(ret[e, 0:half - 1], axis=0)
        return total * (scale * UNITS)

    def take_params():
        w = par_buf.at[pl.ds(0, devices - 1)]
        pltpu.make_async_remote_copy(w, w, par_send, par_recv, device_id=coords(1), device_id_type=MESH).wait_recv()
        par_buf[me] = par_own[...]
        table = par_buf[...].reshape(devices, 128)
        owner = own_ref[...]
        hot = (lax.broadcasted_iota(jnp.int32, (devices, nodes), 0) == owner).astype(F32)
        hot16 = hot.astype(BF16)
        earlier = (lax.broadcasted_iota(jnp.int32, (nodes, nodes), 0) < lax.broadcasted_iota(jnp.int32, (nodes, nodes), 1))
        before = dot(hot16, earlier.astype(F32).astype(BF16), ((1,), (0,)))
        rank = jnp.sum(before * hot, axis=0, keepdims=True)
        rows = sum(dot(p, hot16, ((0,), (0,))) for p in split3(table))
        place = lax.broadcasted_iota(jnp.int32, (128, nodes), 0)
        base = rank.astype(jnp.int32) * FIELDS
        rows = jnp.where((place >= base) & (place < base + FIELDS), rows, 0.0)
        fold = ((lax.broadcasted_iota(jnp.int32, (16, 128), 1) % FIELDS) == lax.broadcasted_iota(jnp.int32, (16, 128), 0))
        fold = fold.astype(F32).astype(BF16)
        prm[...] = sum(dot(fold, p, ((1,), (0,))) for p in split3(rows))

    def membrane(x):
        length, modulus, bend = prm[0:6], prm[6:8], prm[8:11]
        index = nbr_ref[...]
        index = jnp.concatenate([index, index[:4]], axis=0)
        edges = []
        for c in range(3):
            halves = []
            for h in range(nodes // 128):
                where = index[:, h * 128:(h + 1) * 128]
                low = lax.rem(where, 128)
                got = None
                for s in range(nodes // 128):
                    pool = jnp.broadcast_to(x[c:c + 1, s * 128:(s + 1) * 128], (16, 128))
                    one = jnp.concatenate([jnp.take_along_axis(pool[k:k + 8], low[k:k + 8], axis=1) for k in (0, 8)], axis=0)
                    got = one if got is None else jnp.where(where >= s * 128, one, got)
                halves.append(got)
            edges.append(jnp.concatenate(halves, axis=1)[:12] - x[c:c + 1])
        square = edges[0][:6] ** 2 + edges[1][:6] ** 2 + edges[2][:6] ** 2
        stretch = square / (length * length)
        tension = (stretch - 1.0) / (stretch + 1.0) / length
        out = []
        for c in range(3):
            surface = modulus[0:1] * jnp.sum(tension * edges[c][:6], axis=0, keepdims=True)
            near = jnp.sum(edges[c][:6], axis=0, keepdims=True) * (2.0 / 9.0)
            far = jnp.sum(edges[c][6:], axis=0, keepdims=True) * (1.0 / 18.0)
            out.append(surface + modulus[1:2] * (near - far - bend[c:c + 1]))
        return jnp.concatenate(out, axis=0)

    prepare(0)
    pl.semaphore_wait(barrier, devices - 1)
    send_first(0)
    par_own[...] = par_ref[me]

    @pl.loop(0, STEPS)
    def _(e):
        u = velocity(e)
        x = place[...] + TIME_STEP * u
        place[...] = x

        @pl.when(e == 0)
        def _():
            take_params()

        blk[e + 1] = pack(x * UNITS, membrane(x))
        send_first(e + 1)
        prepare(e + 1)

    x_out[...] = place[...]
    v_out[...] = velocity(STEPS)
    for e in range(STEPS + 1):
        w = buf.at[e, pl.ds(1, half), pl.ds(0, 6)]
        pltpu.make_async_remote_copy(w, w, send_sem.at[e], recv_sem.at[e, 0], device_id=coords(1), device_id_type=MESH).wait_send()
        w = ret.at[e, pl.ds(0, half - 1)]
        pltpu.make_async_remote_copy(w, w, ret_send.at[e], ret_recv.at[e], device_id=coords(1), device_id_type=MESH).wait_send()
    w = par_buf.at[pl.ds(0, devices - 1)]
    pltpu.make_async_remote_copy(w, w, par_send, par_recv, device_id=coords(1), device_id_type=MESH).wait_send()


def solution(mesh):
    n_tgt, n_src = mesh.shape["tgt"], mesh.shape["src"]
    devices = n_tgt * n_src

    def body(positions, forces, neighbours, patch_owner, rest_length, moduli, rest_bend):
        nodes = positions.shape[1]
        capacity = rest_length.shape[1] // devices
        fields = jnp.concatenate([rest_length, moduli, rest_bend, jnp.zeros_like(moduli[:1])], axis=0)
        table = fields.reshape(FIELDS, devices, capacity).transpose(1, 2, 0).reshape(devices, 1, capacity * FIELDS)
        table = jnp.pad(table, ((0, 0), (0, 0), (0, 128 - capacity * FIELDS)))
        vmem = pl.BlockSpec(memory_space=pltpu.VMEM)
        return pl.pallas_call(
            functools.partial(kernel, n_src, devices, nodes, capacity, 1.0 / math.sqrt(nodes * devices)),
            name="stokes",
            out_shape=(jax.ShapeDtypeStruct((3, nodes), F32), jax.ShapeDtypeStruct((3, nodes), F32)),
            in_specs=[vmem] * 5,
            out_specs=(vmem, vmem),
            scratch_shapes=[
                pltpu.VMEM((STEPS + 1, devices // 2 + 1, 8, nodes), F32),
                pltpu.VMEM((STEPS + 1, 8, nodes), F32),
                pltpu.VMEM((STEPS + 1, devices // 2, 3, nodes), F32),
                pltpu.VMEM((STEPS + 1, devices // 2, 3, nodes), F32),
                pltpu.VMEM((devices, 1, 128), F32),
                pltpu.VMEM((1, 128), F32),
                pltpu.VMEM((16, nodes), F32),
                pltpu.VMEM((3, nodes), F32),
                pltpu.VMEM((3, nodes, 128), F32),
                pltpu.VMEM((2 * nodes, 48), BF16),
                pltpu.VMEM((16, nodes), BF16),
                pltpu.VMEM((2, 16, nodes), BF16),
                pltpu.VMEM((2, 2 * nodes, nodes), F32),
                pltpu.VMEM((3, nodes, 128), F32),
                pltpu.VMEM((16, nodes), F32),
                pltpu.SemaphoreType.DMA((STEPS + 1,)),
                pltpu.SemaphoreType.DMA((STEPS + 1, devices // 4)),
                pltpu.SemaphoreType.DMA((STEPS + 1,)),
                pltpu.SemaphoreType.DMA((STEPS + 1,)),
                pltpu.SemaphoreType.DMA,
                pltpu.SemaphoreType.DMA,
            ],
            compiler_params=pltpu.CompilerParams(collective_id=0, has_side_effects=True, vmem_limit_bytes=48 * 1024 * 1024),
        )(positions, forces, neighbours, patch_owner.reshape(1, nodes), table)

    cut = P(None, ("tgt", "src"))
    return jax.shard_map(
        body,
        mesh=mesh,
        in_specs=(cut, cut, cut, P(("tgt", "src"), None), cut, cut, cut),
        out_specs=(cut, cut),
        check_vma=False,
    )
```
